128 devices in a mesh: wide: 64 (over y, x, z), narrow: 2 (over core).
Axes of the slice: x: 4, y: 4, z: 4, core: 2. Of those that a mesh axis runs over, the one named last changes fastest.
Arguments:
- hidden_in: bfloat16 [8192, 4096], P('wide'), may hold values from -6 to 6
- readout: bfloat16 [8192, 4096], P('wide'), may hold values from -0.09375 to 0.09375
- route_ids: int32 [8192, 8], P('wide'), may hold values from 0 to 63, all different within a row; in each aligned block of 128 rows (0 to 127, 128 to 255, ...) at most 24 rows name the same one
- route_weights: bfloat16 [8192, 8], P('wide'), may hold values from 0.25 to 1
- forget_mask: int32 [8192], P('wide'), may hold values 0 or 1
- gate_proj: bfloat16 [64, 4096, 1536], P('wide', None, 'narrow'), may hold values from -0.09375 to 0.09375
- up_proj: bfloat16 [64, 4096, 1536], P('wide', None, 'narrow'), may hold values from -0.09375 to 0.09375
- adapter_a: bfloat16 [64, 16, 1536], P('wide', None, 'narrow'), may hold values from -0.15625 to 0.15625
- adapter_b: bfloat16 [64, 16, 4096], P('wide'), may hold values from -1.5 to 1.5
Outputs:
- log_ratio: float32 [8192], P('wide')
- grad_a: float32 [64, 16, 1536], P('wide', None, 'narrow')
- grad_b: float32 [64, 16, 4096], P('wide')
The draws below stay inside these ranges and needn't reach their ends.
Inputs may be any that keep to these rules, and one draw needn't show every extreme that they name: `route_ids`: each token names 8 different experts. Among the 128 tokens of one index of wide no expert is named by more than 24 tokens, and in some such blocks one expert is named by exactly 24.
All inputs are finite; a program needn't handle non-finite values. No bound on the sum of `forget_mask` on one device may be relied on, other than what follows from the above.
Results may differ from the reference program's by a relative error of at most 0.027.
Values may be sent and summed in bfloat16 or wider, within the bound.
No kernel may reach another device: no remote copies, remote signals or barrier semaphores. Data moves between devices by JAX's collectives and lax.ppermute only.
A program may use at most 192 MiB of HBM per device.

```python
import math
import jax
import jax.numpy as jnp
import numpy as np
from jax import lax

D = 4096
FF = 1536
TOPK = 8
R = 16
TOK_DEV = 128
EXPERTS = 64
TOKENS = 8192
CAP = 24


def place_ends(values, rng, smallest, top_value):
    shape = values.shape
    spot = [jax.random.randint(jax.random.fold_in(rng, axis), (), 0, shape[axis]) for axis in range(len(shape))]
    values = values.at[tuple(spot)].set(smallest)
    longest = shape.index(max(shape))
    spot[longest] = (spot[longest] + 1) % shape[longest]
    return values.at[tuple(spot)].set(top_value)


def steps_of(stream_key, shape, split, smallest, high):
    loudness, own = 1.0, jax.random.fold_in(stream_key, 6)
    for dim, parts in split:
        heights = jnp.exp(jax.random.uniform(jax.random.fold_in(own, dim), (parts,), jnp.float32, smallest / len(split), high / len(split)))
        loudness = loudness * jnp.repeat(heights, shape[dim] // parts).reshape([-1 if axis == dim else 1 for axis in range(len(shape))])
    return loudness


def deal_out(stream_key, own, number, rows, count, top, most, skew):
    order = jax.random.permutation(stream_key, count)
    packed, ordinary = shares(count, rows * top, most, skew, True), shares(count, rows * top, most, skew, False)
    places = jnp.arange(count)

    def named(tallies, offset_by):
        used = int((tallies > 0).sum())
        fixed = max(1, used // 4)
        moved = fixed + (places - fixed + offset_by * (used - fixed)) % max(1, count - fixed)
        return jnp.zeros((count,), jnp.int32).at[order[jnp.where(places < fixed, places, moved)]].set(jnp.asarray(tallies, jnp.int32))

    tallies = jnp.where(number % 4 == 0, named(packed, number // 4), named(ordinary, number - number // 4 - 1))
    mixed = jax.random.permutation(jax.random.fold_in(own, 3), count)
    donor, taker = mixed[0:count // 2 * 2:2], mixed[1:count // 2 * 2:2]
    slack = jnp.minimum(tallies[donor] - 1, most - tallies[taker]) // 2
    slack = jnp.where((donor == order[0]) | (taker == order[0]) | (tallies[taker] == 0), 0, jnp.maximum(slack, 0))
    moved = jax.random.randint(jax.random.fold_in(own, 4), (count // 2,), 0, 1 << 20) % (slack + 1)
    tallies = tallies.at[donor].add(-moved).at[taker].add(moved)
    items = jnp.searchsorted(jnp.cumsum(tallies), jnp.arange(rows * top), side="right").astype(jnp.int32)
    listing = items.reshape(top, rows).T
    listing = listing[jax.random.permutation(jax.random.fold_in(own, 1), rows)]
    offset_by = jax.random.randint(jax.random.fold_in(own, 2), (rows, 1), 0, top)
    return jnp.take_along_axis(listing, (jnp.arange(top)[None, :] + offset_by) % top, axis=1)


def shares(amount, total, limit, slope, full):
    loads = [(1 << 20) // math.isqrt(rank ** slope) + 1 for rank in range(1, amount + 1)]
    largest = limit if full else min(limit, max(-(-total // amount), total * loads[0] // sum(loads)))
    least = 1 if total - largest >= amount - 1 else 0
    given, surplus = [largest] + [least] * (amount - 1), total - largest - least * (amount - 1)
    while surplus > 0:
        movable = [i for i in range(1, amount) if given[i] < largest] or [i for i in range(1, amount) if given[i] < limit]
        mass, budget = sum([loads[i] for i in movable]), surplus
        for i in movable:
            more = min(limit - given[i], max(1, budget * loads[i] // mass), surplus)
            given[i] = given[i] + more
            surplus = surplus - more
    return np.array(given)


def centred(stream_key, dims, width, most, split=(), kind=jnp.bfloat16):
    level = steps_of(stream_key, dims, split, -0.22, 0.18) if split else 1.0
    array = jax.random.normal(stream_key, dims, jnp.float32) * width * level
    return jnp.minimum(jnp.maximum(array, -most), most).astype(kind)


def setup_inputs(seed: int = 0) -> dict:
    keys = jax.random.split(jax.random.key(seed), 10)
    hidden_in = centred(keys[0], (TOKENS, D), 1.0, 6.0, ((0, 64),))
    readout = centred(keys[1], (TOKENS, D), D ** -0.5, 0.09375, ((0, 64),))
    route_ids_keys = jax.random.split(jax.random.fold_in(keys[2], 1), TOKENS // TOK_DEV)
    route_ids_turns = jax.random.permutation(jax.random.fold_in(keys[2], 3), TOKENS // TOK_DEV)
    route_ids = jax.vmap(lambda own, number: deal_out(jax.random.fold_in(keys[2], 2), own, number, TOK_DEV, EXPERTS, TOPK, CAP, 1))(route_ids_keys, route_ids_turns).reshape((TOKENS, TOPK))
    route_weights = jnp.clip(0.25 + 0.75 * jax.random.uniform(keys[3], (TOKENS, TOPK), jnp.float32) ** steps_of(keys[3], (TOKENS, TOPK), ((0, 64),), -0.2, 0.2), 0.25, 1.0).astype(jnp.bfloat16)
    forget_mask = place_ends((jax.random.randint(keys[4], (TOKENS,), 0, 4) < 3).astype(jnp.int32), jax.random.fold_in(keys[4], 1), 0, 1)
    gate_proj = centred(keys[5], (EXPERTS, D, FF), D ** -0.5, 0.09375, ((0, 64), (2, 2)))
    up_proj = centred(keys[6], (EXPERTS, D, FF), D ** -0.5, 0.09375, ((0, 64), (2, 2)))
    adapter_a = centred(keys[7], (EXPERTS, R, FF), FF ** -0.5, 0.15625, ((0, 64), (2, 2)))
    adapter_b = centred(keys[8], (EXPERTS, R, D), R ** -0.5, 1.5, ((0, 64),))
    return dict(hidden_in=hidden_in, readout=readout, route_ids=route_ids, route_weights=route_weights, forget_mask=forget_mask, gate_proj=gate_proj, up_proj=up_proj, adapter_a=adapter_a, adapter_b=adapter_b)


def slot_tables(block_ids, experts, capacity):
    total = block_ids.shape[0]
    matches = (block_ids[:, None] == jnp.arange(experts, dtype=jnp.int32)[None, :]).astype(jnp.int32)
    earlier = jnp.cumsum(matches, axis=0) - matches
    slot_rank = jnp.sum(earlier * matches, axis=1).astype(jnp.int32)
    slot_place = (block_ids * capacity + slot_rank).astype(jnp.int32)
    slot_owner = jnp.full((experts * capacity,), -1, dtype=jnp.int32).at[slot_place].set(jnp.arange(total, dtype=jnp.int32))
    return slot_place, slot_owner


def reference(hidden_in, readout, route_ids, route_weights, forget_mask, gate_proj, up_proj, adapter_a, adapter_b):
    blocks = TOKENS // TOK_DEV
    per_block = TOK_DEV * TOPK
    block_ids = route_ids.reshape(blocks, per_block).astype(jnp.int32)
    slot_place, slot_owner = jax.vmap(lambda id_row: slot_tables(id_row, EXPERTS, CAP))(block_ids)
    offsets = (jnp.arange(blocks, dtype=jnp.int32) * per_block)[:, None]
    global_owner = jnp.where(slot_owner >= 0, slot_owner + offsets, -1).astype(jnp.int32)
    expert_slots = global_owner.reshape(blocks, EXPERTS, CAP).transpose(1, 0, 2).reshape(EXPERTS, blocks * CAP)

    def forward(inputs):
        slots, w_gate, w_up, down_a, down_b = inputs
        filled = slots >= 0
        token_of = (jnp.maximum(slots, 0) // TOPK).astype(jnp.int32)
        expert_rows = jnp.where(filled[:, None], hidden_in[token_of], jnp.zeros((), hidden_in.dtype))
        pre_gate = jnp.dot(expert_rows, w_gate, preferred_element_type=jnp.float32)
        pre_up = jnp.dot(expert_rows, w_up, preferred_element_type=jnp.float32)
        expert_hidden = (jax.nn.silu(pre_gate) * pre_up).astype(jnp.bfloat16)
        latent = lax.dot_general(expert_hidden, down_a, (((1,), (1,)), ((), ())), preferred_element_type=jnp.float32).astype(jnp.bfloat16)
        deltas = jnp.dot(latent, down_b, preferred_element_type=jnp.float32).astype(jnp.bfloat16)
        scores = jnp.einsum("sd,sd->s", deltas.astype(jnp.float32), readout[token_of].astype(jnp.float32)).astype(jnp.bfloat16)
        return expert_hidden, latent, scores

    hidden_all, latent_all, score_all = lax.map(forward, (expert_slots, gate_proj, up_proj, adapter_a, adapter_b))
    expert_of = slot_place // CAP
    rank_of = slot_place % CAP
    flat_index = (expert_of * (blocks * CAP) + jnp.arange(blocks, dtype=jnp.int32)[:, None] * CAP + rank_of).astype(jnp.int32)
    scores = score_all.reshape(-1)[flat_index.reshape(-1)].reshape(TOKENS, TOPK).astype(jnp.float32)
    gains = route_weights.astype(jnp.float32)
    log_ratio = jnp.sum(gains * scores, axis=1)
    coefficient = 2.0 * forget_mask.astype(jnp.float32) * jax.nn.sigmoid(log_ratio)
    slot_weight = (gains * coefficient[:, None]).astype(jnp.bfloat16).reshape(-1)

    def backward(inputs):
        slots, down_b, expert_hidden, latent = inputs
        filled = slots >= 0
        safe_slots = jnp.maximum(slots, 0).astype(jnp.int32)
        token_of = (safe_slots // TOPK).astype(jnp.int32)
        weights = jnp.where(filled, slot_weight[safe_slots], jnp.zeros((), slot_weight.dtype))
        slot_cot = (weights.astype(jnp.float32)[:, None] * readout[token_of].astype(jnp.float32)).astype(jnp.bfloat16)
        grad_b = lax.dot_general(latent, slot_cot, (((0,), (0,)), ((), ())), preferred_element_type=jnp.float32)
        back_latent = lax.dot_general(slot_cot, down_b, (((1,), (1,)), ((), ())), preferred_element_type=jnp.float32).astype(jnp.bfloat16)
        grad_a = lax.dot_general(back_latent, expert_hidden, (((0,), (0,)), ((), ())), preferred_element_type=jnp.float32)
        return grad_a, grad_b

    grad_a, grad_b = lax.map(backward, (expert_slots, adapter_b, hidden_all, latent_all))
    return log_ratio, grad_a, grad_b
```

```python
import functools

import jax
import jax.numpy as jnp
from jax import lax
from jax.experimental import pallas as pl
from jax.experimental.pallas import tpu as pltpu
from jax.sharding import PartitionSpec as P

F32 = jnp.float32
BF16 = jnp.bfloat16
ROWS = 8
PARTS = (16, 8)


def iota(shape, dim):
    return lax.broadcasted_iota(jnp.int32, shape, dim)


def ones_where(condition, dtype=BF16):
    return jnp.where(condition, 1.0, 0.0).astype(dtype)


def dot(a, b, dims=((1,), (0,)), precision=None):
    return lax.dot_general(a, b, (dims, ((), ())), precision=precision, preferred_element_type=F32)


def transposed(block):
    tokens = block.shape[0]
    eye = ones_where(iota((tokens, tokens), 0) == iota((tokens, tokens), 1))
    return dot(block.astype(BF16), eye, ((0,), (0,)))


def slot_of_token(ids, experts):
    tokens, picks = ids.shape
    ids_t = transposed(ids.astype(F32))
    expert = iota((experts, tokens), 0).astype(F32)
    match = jnp.zeros((experts, tokens), F32)
    for k in range(picks):
        match = match + jnp.where(ids_t[k : k + 1, :] == expert, 1.0, 0.0)
    before = ones_where(iota((tokens, tokens), 0) < iota((tokens, tokens), 1))
    rank = dot(match.astype(BF16), before)
    return jnp.where(match > 0.0, rank, -1.0), ids_t


def spread(groups, slots=ROWS):
    shape = (groups * slots, groups)
    return ones_where(iota(shape, 0) // slots == iota(shape, 1))


def gathered(groups):
    shape = (groups, groups * ROWS)
    return ones_where(iota(shape, 1) // ROWS == iota(shape, 0))


def own_lanes(rows, rank, slots=ROWS):
    shape = (rows, slots * rank)
    return iota(shape, 0) % slots == iota(shape, 1) // rank


def one_hot_slots(slots, first, count=ROWS):
    rows = slots.shape[0] * count
    wide = dot(spread(slots.shape[0], count), slots.astype(BF16))
    wanted = (iota((rows, slots.shape[1]), 0) % count + first).astype(F32)
    return jnp.where(wide == wanted, 1.0, 0.0)


def dispatch_body(experts, first, count, core_ref, ids_ref, rows_ref, out_ref, hot_ref):
    @pl.when(pl.program_id(0) == 0)
    def _():
        slots, _unused = slot_of_token(ids_ref[...], experts)
        hot_ref[...] = one_hot_slots(slots, first, count).astype(BF16)

    out_ref[...] = dot(hot_ref[...], rows_ref[...]).astype(BF16)


def dispatch(core, ids, rows, experts, first, count):
    tokens, features = rows.shape
    half = features // 2
    block = min(512, half)
    steps = half // block
    sent = experts * count
    return pl.pallas_call(
        functools.partial(dispatch_body, experts, first, count),
        grid_spec=pltpu.PrefetchScalarGridSpec(
            num_scalar_prefetch=1,
            grid=(steps,),
            in_specs=[
                pl.BlockSpec(ids.shape, lambda n, c: (0, 0)),
                pl.BlockSpec((tokens, block), lambda n, c: (0, c[0] * steps + n)),
            ],
            out_specs=pl.BlockSpec((sent, block), lambda n, c: (0, n)),
            scratch_shapes=[pltpu.VMEM((sent, tokens), BF16)],
        ),
        out_shape=jax.ShapeDtypeStruct((sent, half), BF16),
        cost_estimate=pl.CostEstimate(
            flops=2 * sent * tokens * half, bytes_accessed=2 * sent * half, transcendentals=0
        ),
        compiler_params=pltpu.CompilerParams(vmem_limit_bytes=24 * 1024 * 1024),
        name="dispatch_rows",
    )(core, ids, rows)


def experts_body(groups, pairs, count, steps, last, core_ref, own_ref, other_ref, go_ref, gx_ref, uo_ref, ux_ref, a_ref, *refs):
    before_refs, (hid_ref, lat_ref, acc_ref) = refs[:-3], refs[-3:]
    n = pl.program_id(0)
    own, other = own_ref[...], other_ref[...]
    gate = dot(own, go_ref[0]) + dot(other, gx_ref[0])
    up = dot(own, uo_ref[0]) + dot(other, ux_ref[0])
    hidden = (gate / (1.0 + jnp.exp(-gate)) * up).astype(BF16)
    hid_ref[...] = hidden
    rank = a_ref.shape[1]
    tiled = jnp.concatenate([a_ref[0]] * count, axis=0)
    part = dot(hidden, tiled, ((1,), (1,)))

    @pl.when(n == 0)
    def _():
        acc_ref[...] = part

    @pl.when(n > 0)
    def _():
        acc_ref[...] = acc_ref[...] + part

    @pl.when(n == steps - 1)
    def _():
        rows = groups * count
        mine = jnp.where(own_lanes(rows, rank, count), acc_ref[...], 0.0).astype(BF16)
        shape = (groups * pairs, rows)
        both = ones_where(iota(shape, 1) // count == iota(shape, 0) // pairs)
        now = dot(both, mine).astype(BF16)
        if last:
            width = ROWS * rank
            pieces = [ref[...] for ref in before_refs] + [now]
            at = 0
            for piece in pieces:
                for c in range(piece.shape[1] // width):
                    lat_ref[:, at, :] = piece[:, c * width : (c + 1) * width]
                    at += 1
            for c in range(at, ROWS):
                lat_ref[:, c, :] = jnp.zeros((groups * pairs, width), BF16)
        else:
            lat_ref[...] = now


def experts_forward(core, own, other, gate, up, adapter_a, before, groups, pairs, last):
    rows, half = own.shape
    count = rows // groups
    hidden_units = gate.shape[2]
    rank = adapter_a.shape[1]
    block = min(256, hidden_units)
    steps = hidden_units // block
    width = count * rank
    mine = pl.BlockSpec((1, half, block), lambda n, c: (0, c[0], n))
    theirs = pl.BlockSpec((1, half, block), lambda n, c: (0, 1 - c[0], n))
    whole = pl.BlockSpec((rows, half), lambda n, c: (0, 0))
    in_specs = [whole, whole, mine, theirs, mine, theirs, pl.BlockSpec((1, rank, block), lambda n, c: (0, 0, n))]
    in_specs += [pl.BlockSpec(x.shape, lambda n, c: (0, 0)) for x in before]
    out = (groups * pairs, ROWS, ROWS * rank) if last else (groups * pairs, width)
    return pl.pallas_call(
        functools.partial(experts_body, groups, pairs, count, steps, last),
        grid_spec=pltpu.PrefetchScalarGridSpec(
            num_scalar_prefetch=1,
            grid=(steps,),
            in_specs=in_specs,
            out_specs=[
                pl.BlockSpec((rows, block), lambda n, c: (0, n)),
                pl.BlockSpec(out, lambda n, c: (0,) * len(out)),
            ],
            scratch_shapes=[pltpu.VMEM((rows, width), F32)],
        ),
        out_shape=[
            jax.ShapeDtypeStruct((rows, hidden_units), BF16),
            jax.ShapeDtypeStruct(out, BF16),
        ],
        cost_estimate=pl.CostEstimate(
            flops=8 * rows * half * hidden_units,
            bytes_accessed=8 * half * hidden_units + 4 * rows * half,
            transcendentals=rows * hidden_units,
        ),
        compiler_params=pltpu.CompilerParams(vmem_limit_bytes=48 * 1024 * 1024),
        name="experts_forward",
    )(core, own, other, gate, gate, up, up, adapter_a, *before)


def project_body(experts, chunks, core_ref, ids_ref, readout_ref, adapters_ref, out_ref):
    rank = adapters_ref.shape[0] // experts
    rows = experts * ROWS
    slots, _unused = slot_of_token(ids_ref[...], experts)
    every = dot(readout_ref[...], adapters_ref[...], ((1,), (1,))).astype(BF16)
    width = experts * rank
    own_expert = iota((rows, width), 0) // ROWS == iota((rows, width), 1) // rank
    fold = ones_where(iota((width, ROWS * rank), 0) % rank == iota((width, ROWS * rank), 1) % rank)
    lanes = own_lanes(rows, rank)
    for c in range(chunks):
        hot = one_hot_slots(slots, c * ROWS).astype(BF16)
        picked = jnp.where(own_expert, dot(hot, every), 0.0).astype(BF16)
        placed = jnp.where(lanes, dot(picked, fold), 0.0).astype(BF16)
        out_ref[:, c * ROWS * rank : (c + 1) * ROWS * rank] = dot(gathered(experts), placed)


def project(core, ids, readout, adapters, experts, chunks):
    tokens, features = readout.shape
    half = features // 2
    rank = adapters.shape[0] // experts
    return pl.pallas_call(
        functools.partial(project_body, experts, chunks),
        grid_spec=pltpu.PrefetchScalarGridSpec(
            num_scalar_prefetch=1,
            grid=(1,),
            in_specs=[
                pl.BlockSpec(ids.shape, lambda n, c: (0, 0)),
                pl.BlockSpec((tokens, half), lambda n, c: (0, c[0])),
                pl.BlockSpec(adapters.shape, lambda n, c: (0, 0)),
            ],
            out_specs=pl.BlockSpec((experts, chunks * ROWS * rank), lambda n, c: (0, 0)),
        ),
        out_shape=jax.ShapeDtypeStruct((experts, chunks * ROWS * rank), F32),
        compiler_params=pltpu.CompilerParams(vmem_limit_bytes=48 * 1024 * 1024),
        name="project_readout",
    )(core, ids, readout, adapters)


def weigh_body(experts, pairs, chunks, core_ref, ids_ref, gains_ref, mask_ref, latent_ref, own_ref, other_ref, readout_ref, log_ref, out_ref, lift_ref):
    tokens, picks = ids_ref.shape
    width = latent_ref.shape[2]
    rank = width // ROWS
    rows = experts * ROWS
    half = readout_ref.shape[1]

    @pl.when(pl.program_id(0) == 0)
    def _():
        slots, ids_t = slot_of_token(ids_ref[...], experts)
        gains_t = transposed(gains_ref[...])
        expert = iota((experts, tokens), 0).astype(F32)
        gains = jnp.zeros((experts, tokens), F32)
        for k in range(picks):
            gains = gains + jnp.where(ids_t[k : k + 1, :] == expert, gains_t[k : k + 1, :], 0.0)
        spread_rows = spread(experts)
        lanes = own_lanes(rows, rank)
        first = iota((rows, width), 1) % rank == 0
        shape = (experts, experts * pairs)
        both = ones_where(iota(shape, 1) // pairs == iota(shape, 0))
        same = ones_where(iota((width, width), 0) // rank == iota((width, width), 1) // rank, F32)
        wide_gains = dot(spread_rows, gains.astype(BF16))
        hots, latents, projections = [], [], []
        total = jnp.zeros((1, tokens), F32)
        for c in range(chunks):
            span = slice(c * width, (c + 1) * width)
            latent = dot(both, latent_ref[:, c, :]).astype(BF16).astype(F32)
            projection = own_ref[:, span] + other_ref[:, span]
            score = dot(latent * projection, same, precision=lax.Precision.HIGHEST).astype(BF16)
            column = jnp.sum(
                jnp.where(lanes & first, dot(spread_rows, score), 0.0), axis=1, keepdims=True
            )
            hot = one_hot_slots(slots, c * ROWS)
            total = total + jnp.sum(hot * wide_gains * column, axis=0, keepdims=True)
            hots.append(hot)
            latents.append(latent)
            projections.append(projection)
        log_ref[...] = total
        coefficient = 2.0 * mask_ref[...].astype(F32) / (1.0 + jnp.exp(-total))
        weight = (gains * coefficient).astype(BF16)
        wide_weight = dot(spread_rows, weight)
        every = experts * rank
        tile = ones_where(iota((width, every), 0) % rank == iota((width, every), 1) % rank)
        own_expert = iota((rows, every), 0) // ROWS == iota((rows, every), 1) // rank
        lift = jnp.zeros((every, tokens), F32)
        out_ref[:, :, half:] = jnp.zeros((experts, rank, width), BF16)
        for c in range(chunks):
            column = jnp.sum(hots[c] * wide_weight, axis=1, keepdims=True)
            placed = jnp.where(lanes, column, 0.0).astype(BF16)
            slot_weight = dot(gathered(experts), placed)
            out_ref[:, c, half:] = (slot_weight * projections[c]).astype(BF16)
            weighted = (slot_weight * latents[c]).astype(BF16)
            weighted = jnp.where(lanes, dot(spread_rows, weighted), 0.0).astype(BF16)
            weighted = jnp.where(own_expert, dot(weighted, tile), 0.0).astype(BF16)
            lift = lift + dot(weighted, hots[c].astype(BF16), ((0,), (0,)))
        lift_ref[...] = lift.astype(BF16)

    block = 512
    for n in range(half // block):
        part = dot(lift_ref[...], readout_ref[:, n * block : (n + 1) * block]).astype(BF16)
        out_ref[:, :, n * block : (n + 1) * block] = part.reshape(experts, rank, block)


def weigh(core, ids, gains, mask, latents, own, other, readout, experts, pairs, chunks):
    tokens = ids.shape[0]
    half = readout.shape[1] // pairs
    width = latents.shape[2]
    rank = width // ROWS
    full = lambda shape: pl.BlockSpec(shape, lambda n, c: (0,) * len(shape))
    out = (experts, rank, half + width)
    return pl.pallas_call(
        functools.partial(weigh_body, experts, pairs, chunks),
        grid_spec=pltpu.PrefetchScalarGridSpec(
            num_scalar_prefetch=1,
            grid=(1,),
            in_specs=[
                full(ids.shape),
                full(gains.shape),
                full(mask.shape),
                full(latents.shape),
                full(own.shape),
                full(other.shape),
                pl.BlockSpec((tokens, half), lambda n, c: (0, c[0])),
            ],
            out_specs=[full((1, tokens)), full(out)],
            scratch_shapes=[pltpu.VMEM((experts * rank, tokens), BF16)],
        ),
        out_shape=[jax.ShapeDtypeStruct((1, tokens), F32), jax.ShapeDtypeStruct(out, BF16)],
        compiler_params=pltpu.CompilerParams(vmem_limit_bytes=40 * 1024 * 1024),
        name="weigh_tokens",
    )(core, ids, gains, mask, latents, own, other, readout)


def gradients_body(groups, packed_ref, *refs):
    hid_refs, (grad_a_ref, grad_b_ref) = refs[:-2], refs[-2:]
    rank, half = grad_b_ref.shape
    block = 256
    for n in range(half // block):
        span = slice(n * block, (n + 1) * block)
        grad_b_ref[:, span] = jnp.sum(packed_ref[:, :, span].astype(F32), axis=0)
    result = jnp.zeros(grad_a_ref.shape, F32)
    at = 0
    for hid_ref in hid_refs:
        rows = hid_ref.shape[0]
        count = rows // groups
        pieces = [packed_ref[:, at + c, half:] for c in range(count // ROWS)]
        at += count // ROWS
        back = dot(spread(groups, count), jnp.concatenate(pieces, axis=1))
        back = jnp.where(own_lanes(rows, rank, count), back, 0.0).astype(BF16)
        total = dot(back, hid_ref[...], ((0,), (0,)))
        for s in range(count):
            result = result + total[s * rank : (s + 1) * rank]
    grad_a_ref[...] = result


def gradients(packed, hidden, rank):
    groups = packed.shape[0]
    half = packed.shape[2] - ROWS * rank
    hidden_units = hidden[0].shape[1]
    return pl.pallas_call(
        functools.partial(gradients_body, groups),
        out_shape=[
            jax.ShapeDtypeStruct((rank, hidden_units), F32),
            jax.ShapeDtypeStruct((rank, half), F32),
        ],
        compiler_params=pltpu.CompilerParams(vmem_limit_bytes=40 * 1024 * 1024),
        name="adapter_gradients",
    )(packed, *hidden)


def swap(payload):
    return lax.ppermute(payload, "narrow", [(0, 1), (1, 0)])


def exchange(payload):
    return lax.all_to_all(payload, "wide", split_axis=0, concat_axis=0, tiled=True)


def on_device(
    hidden_in,
    readout,
    route_ids,
    route_weights,
    forget_mask,
    gate_proj,
    up_proj,
    adapter_a,
    adapter_b,
):
    groups = lax.axis_size("wide")
    pairs = lax.axis_size("narrow")
    tokens, picks = route_ids.shape
    features = hidden_in.shape[1]
    half = features // pairs
    rank = adapter_a.shape[1]
    chunks = sum(PARTS) // ROWS
    side = lax.axis_index("narrow")
    core = side.reshape(1).astype(jnp.int32)

    own_b = lax.dynamic_slice_in_dim(adapter_b[0], side * half, half, 1)
    own_b, route_ids = lax.optimization_barrier((own_b, route_ids))
    adapters = lax.all_gather(own_b, "wide", axis=0, tiled=True)

    own, first = [], 0
    for count in PARTS:
        sent = dispatch(core, route_ids, hidden_in, groups, first, count)
        own.append(exchange(sent.reshape(groups, count, half)).reshape(groups * count, half))
        first += count

    hidden, latents = [], []
    for part, x in enumerate(own):
        if hidden:
            x, hidden[-1] = lax.optimization_barrier((x, hidden[-1]))
        acts, sums = experts_forward(
            core, x, swap(x), gate_proj, up_proj, adapter_a, latents, groups, pairs, part == len(own) - 1
        )
        hidden.append(acts)
        latents.append(sums)
    projections = project(core, route_ids, readout, adapters, groups, chunks)
    home_latents = lax.all_to_all(
        latents[-1], ("wide", "narrow"), split_axis=0, concat_axis=0, tiled=True
    )
    log_ratio, packed = weigh(
        core,
        route_ids,
        route_weights,
        forget_mask.reshape(1, tokens),
        home_latents,
        projections,
        swap(projections),
        readout,
        groups,
        pairs,
        chunks,
    )
    grad_a, part_b = gradients(exchange(packed), hidden, rank)
    other_b = swap(part_b)
    grad_b = jnp.where(
        side == 0,
        jnp.concatenate([part_b, other_b], axis=1),
        jnp.concatenate([other_b, part_b], axis=1),
    )
    return (log_ratio.reshape(tokens), grad_a[None], grad_b[None])


def solution(mesh):
    return jax.shard_map(
        on_device,
        mesh=mesh,
        in_specs=(
            P("wide", None),
            P("wide", None),
            P("wide", None),
            P("wide", None),
            P("wide"),
            P("wide", None, "narrow"),
            P("wide", None, "narrow"),
            P("wide", None, "narrow"),
            P("wide", None, None),
        ),
        out_specs=(P("wide"), P("wide", None, "narrow"), P("wide", None, None)),
        check_vma=False,
    )
```

```python
import functools

import jax
import jax.numpy as jnp
from jax import lax
from jax.experimental import pallas as pl
from jax.experimental.pallas import tpu as pltpu
from jax.sharding import PartitionSpec as P

F32 = jnp.float32
BF16 = jnp.bfloat16
ROWS = 8
LINE = 4
PARTS = (16, 8)


def iota(shape, dim):
    return lax.broadcasted_iota(jnp.int32, shape, dim)


def ones_where(condition, dtype=BF16):
    return jnp.where(condition, 1.0, 0.0).astype(dtype)


def dot(a, b, dims=((1,), (0,)), precision=None):
    return lax.dot_general(a, b, (dims, ((), ())), precision=precision, preferred_element_type=F32)


def slot_of_token(ids_t, experts):
    picks, tokens = ids_t.shape
    match = matched(ids_t, jnp.ones((picks, tokens), F32), experts)
    before = ones_where(iota((tokens, tokens), 0) < iota((tokens, tokens), 1))
    rank = dot(match.astype(BF16), before)
    return jnp.where(match > 0.0, rank, -1.0)


def matched(ids_t, values_t, experts):
    picks, tokens = ids_t.shape
    expert = iota((experts, tokens), 0)
    result = jnp.zeros((experts, tokens), F32)
    for k in range(picks):
        result = result + jnp.where(ids_t[k : k + 1, :] == expert, values_t[k : k + 1, :], 0.0)
    return result


def spread(groups, slots=ROWS):
    shape = (groups * slots, groups)
    return ones_where(iota(shape, 0) // slots == iota(shape, 1))


def gathered(groups):
    shape = (groups, groups * ROWS)
    return ones_where(iota(shape, 1) // ROWS == iota(shape, 0))


def own_lanes(rows, rank, slots=ROWS):
    shape = (rows, slots * rank)
    return iota(shape, 0) % slots == iota(shape, 1) // rank


def one_hot_slots(slots, first, count=ROWS):
    rows = slots.shape[0] * count
    wide = dot(spread(slots.shape[0], count), slots.astype(BF16))
    wanted = (iota((rows, slots.shape[1]), 0) % count + first).astype(F32)
    return jnp.where(wide == wanted, 1.0, 0.0)


def dispatch_body(experts, core_ref, ids_ref, rows_ref, *refs):
    out_refs, hot_refs = refs[: len(PARTS)], refs[len(PARTS) :]

    @pl.when(pl.program_id(0) == 0)
    def _():
        slots = slot_of_token(ids_ref[...], experts)
        first = 0
        for hot_ref, count in zip(hot_refs, PARTS):
            hot_ref[...] = one_hot_slots(slots, first, count).astype(BF16)
            first += count

    rows = rows_ref[...]
    for out_ref, hot_ref in zip(out_refs, hot_refs):
        out_ref[...] = dot(hot_ref[...], rows).astype(BF16)


def dispatch(core, ids_t, rows, experts):
    tokens, features = rows.shape
    half = features // 2
    block = min(512, half)
    steps = half // block
    sizes = [experts * count for count in PARTS]
    return pl.pallas_call(
        functools.partial(dispatch_body, experts),
        grid_spec=pltpu.PrefetchScalarGridSpec(
            num_scalar_prefetch=1,
            grid=(steps,),
            in_specs=[
                pl.BlockSpec(ids_t.shape, lambda n, c: (0, 0)),
                pl.BlockSpec((tokens, block), lambda n, c: (0, c[0] * steps + n)),
            ],
            out_specs=[pl.BlockSpec((size, block), lambda n, c: (0, n)) for size in sizes],
            scratch_shapes=[pltpu.VMEM((size, tokens), BF16) for size in sizes],
        ),
        out_shape=[jax.ShapeDtypeStruct((size, half), BF16) for size in sizes],
        cost_estimate=pl.CostEstimate(
            flops=2 * sum(sizes) * tokens * half,
            bytes_accessed=2 * sum(sizes) * half,
            transcendentals=0,
        ),
        compiler_params=pltpu.CompilerParams(vmem_limit_bytes=24 * 1024 * 1024),
        name="dispatch_rows",
    )(core, ids_t, rows)


def experts_body(groups, pairs, count, steps, last, core_ref, own_ref, other_ref, go_ref, gx_ref, uo_ref, ux_ref, a_ref, *refs):
    before_refs, (hid_ref, lat_ref, acc_ref) = refs[:-3], refs[-3:]
    n = pl.program_id(0)
    own, other = own_ref[...], other_ref[...]
    gate = dot(own, go_ref[0]) + dot(other, gx_ref[0])
    up = dot(own, uo_ref[0]) + dot(other, ux_ref[0])
    hidden = (gate / (1.0 + jnp.exp(-gate)) * up).astype(BF16)
    hid_ref[...] = hidden
    rank = a_ref.shape[1]
    tiled = jnp.concatenate([a_ref[0]] * count, axis=0)
    part = dot(hidden, tiled, ((1,), (1,)))

    @pl.when(n == 0)
    def _():
        acc_ref[...] = part

    @pl.when(n > 0)
    def _():
        acc_ref[...] = acc_ref[...] + part

    @pl.when(n == steps - 1)
    def _():
        rows = groups * count
        mine = jnp.where(own_lanes(rows, rank, count), acc_ref[...], 0.0).astype(BF16)
        shape = (groups * pairs, rows)
        both = ones_where(iota(shape, 1) // count == iota(shape, 0) // pairs)
        now = dot(both, mine).astype(BF16)
        if last:
            width = ROWS * rank
            pieces = [ref[...] for ref in before_refs] + [now]
            at = 0
            for piece in pieces:
                for c in range(piece.shape[1] // width):
                    lat_ref[:, at, :] = piece[:, c * width : (c + 1) * width]
                    at += 1
            for c in range(at, ROWS):
                lat_ref[:, c, :] = jnp.zeros((groups * pairs, width), BF16)
        else:
            lat_ref[...] = now


def experts_forward(core, own, other, gate, up, adapter_a, before, groups, pairs, last):
    rows, half = own.shape
    count = rows // groups
    hidden_units = gate.shape[2]
    rank = adapter_a.shape[1]
    block = min(256, hidden_units)
    steps = hidden_units // block
    width = count * rank
    mine = pl.BlockSpec((1, half, block), lambda n, c: (0, c[0], n))
    theirs = pl.BlockSpec((1, half, block), lambda n, c: (0, 1 - c[0], n))
    whole = pl.BlockSpec((rows, half), lambda n, c: (0, 0))
    in_specs = [whole, whole, mine, theirs, mine, theirs, pl.BlockSpec((1, rank, block), lambda n, c: (0, 0, n))]
    in_specs += [pl.BlockSpec(x.shape, lambda n, c: (0, 0)) for x in before]
    out = (groups * pairs, ROWS, ROWS * rank) if last else (groups * pairs, width)
    return pl.pallas_call(
        functools.partial(experts_body, groups, pairs, count, steps, last),
        grid_spec=pltpu.PrefetchScalarGridSpec(
            num_scalar_prefetch=1,
            grid=(steps,),
            in_specs=in_specs,
            out_specs=[
                pl.BlockSpec((rows, block), lambda n, c: (0, n)),
                pl.BlockSpec(out, lambda n, c: (0,) * len(out)),
            ],
            scratch_shapes=[pltpu.VMEM((rows, width), F32)],
        ),
        out_shape=[
            jax.ShapeDtypeStruct((rows, hidden_units), BF16),
            jax.ShapeDtypeStruct(out, BF16),
        ],
        cost_estimate=pl.CostEstimate(
            flops=8 * rows * half * hidden_units,
            bytes_accessed=8 * half * hidden_units + 4 * rows * half,
            transcendentals=rows * hidden_units,
        ),
        compiler_params=pltpu.CompilerParams(vmem_limit_bytes=48 * 1024 * 1024),
        name="experts_forward",
    )(core, own, other, gate, gate, up, up, adapter_a, *before)


def project_body(*refs):
    readout_refs, adapter_refs, out_refs = refs[:LINE], refs[LINE : 2 * LINE], refs[2 * LINE :]
    adapters = jnp.concatenate([ref[...] for ref in adapter_refs], axis=0)
    for readout_ref, out_ref in zip(readout_refs, out_refs):
        out_ref[...] = dot(readout_ref[...], adapters, ((1,), (1,))).astype(BF16)


def project(readouts, adapters):
    tokens, half = readouts[0].shape
    width = LINE * adapters[0].shape[0]
    return pl.pallas_call(
        project_body,
        out_shape=[jax.ShapeDtypeStruct((tokens, width), BF16)] * LINE,
        cost_estimate=pl.CostEstimate(
            flops=2 * LINE * tokens * width * half,
            bytes_accessed=2 * half * (LINE * tokens + width),
            transcendentals=0,
        ),
        compiler_params=pltpu.CompilerParams(vmem_limit_bytes=24 * 1024 * 1024),
        name="project_readout",
    )(*readouts, *adapters)


def pick_body(experts, chunks, place_ref, ids_ref, *refs):
    piece_refs, out_ref = refs[:LINE], refs[LINE]
    slots = slot_of_token(ids_ref[...], experts)
    part = experts // LINE
    every = piece_refs[0].shape[1]
    rank = every // part
    rows, width = part * ROWS, ROWS * rank
    own_expert = iota((rows, every), 0) // ROWS == iota((rows, every), 1) // rank
    fold = ones_where(iota((every, width), 0) % rank == iota((every, width), 1) % rank)
    lanes = own_lanes(rows, rank)
    shape = (rows, experts)
    for c in range(chunks):
        total = jnp.zeros((experts, width), F32)
        for step, piece_ref in enumerate(piece_refs):
            back = iota(shape, 0) // ROWS
            expert = (place_ref[0] - back // LINE) % LINE
            expert = expert * LINE + (place_ref[1] - back % LINE) % LINE
            expert = expert * LINE + (place_ref[2] + step) % LINE
            pick = ones_where(expert == iota(shape, 1))
            wide = dot(pick, slots.astype(BF16))
            wanted = (iota(wide.shape, 0) % ROWS + c * ROWS).astype(F32)
            picked = dot(ones_where(wide == wanted), piece_ref[...])
            picked = jnp.where(own_expert, picked, 0.0).astype(BF16)
            placed = jnp.where(lanes, dot(picked, fold), 0.0).astype(BF16)
            total = total + dot(pick, placed, ((0,), (0,)))
        out_ref[:, c * width : (c + 1) * width] = total


def pick(place, ids_t, pieces, experts, chunks):
    full = lambda shape: pl.BlockSpec(shape, lambda n, c: (0,) * len(shape))
    rank = pieces[0].shape[1] * LINE // experts
    out = (experts, chunks * ROWS * rank)
    return pl.pallas_call(
        functools.partial(pick_body, experts, chunks),
        grid_spec=pltpu.PrefetchScalarGridSpec(
            num_scalar_prefetch=1,
            grid=(1,),
            in_specs=[full(ids_t.shape)] + [full(x.shape) for x in pieces],
            out_specs=full(out),
        ),
        out_shape=jax.ShapeDtypeStruct(out, F32),
        compiler_params=pltpu.CompilerParams(vmem_limit_bytes=24 * 1024 * 1024),
        name="pick_projections",
    )(place, ids_t, *pieces)


def weigh_body(experts, pairs, chunks, ids_ref, gains_ref, mask_ref, latent_ref, own_ref, other_ref, readout_ref, log_ref, out_ref, lift_ref):
    tokens = ids_ref.shape[1]
    width = latent_ref.shape[2]
    rank = width // ROWS
    rows = experts * ROWS
    half = readout_ref.shape[1]

    @pl.when(pl.program_id(0) == 0)
    def _():
        slots = slot_of_token(ids_ref[...], experts)
        gains = matched(ids_ref[...], gains_ref[...].astype(F32), experts)
        spread_rows = spread(experts)
        lanes = own_lanes(rows, rank)
        first = iota((rows, width), 1) % rank == 0
        shape = (experts, experts * pairs)
        both = ones_where(iota(shape, 1) // pairs == iota(shape, 0))
        same = ones_where(iota((width, width), 0) // rank == iota((width, width), 1) // rank, F32)
        wide_gains = dot(spread_rows, gains.astype(BF16))
        hots, latents, projections = [], [], []
        total = jnp.zeros((1, tokens), F32)
        for c in range(chunks):
            span = slice(c * width, (c + 1) * width)
            latent = dot(both, latent_ref[:, c, :]).astype(BF16).astype(F32)
            projection = own_ref[:, span] + other_ref[:, span]
            score = dot(latent * projection, same, precision=lax.Precision.HIGHEST).astype(BF16)
            column = jnp.sum(
                jnp.where(lanes & first, dot(spread_rows, score), 0.0), axis=1, keepdims=True
            )
            hot = one_hot_slots(slots, c * ROWS)
            total = total + jnp.sum(hot * wide_gains * column, axis=0, keepdims=True)
            hots.append(hot)
            latents.append(latent)
            projections.append(projection)
        log_ref[...] = total
        coefficient = 2.0 * mask_ref[...].astype(F32) / (1.0 + jnp.exp(-total))
        weight = (gains * coefficient).astype(BF16)
        wide_weight = dot(spread_rows, weight)
        every = experts * rank
        tile = ones_where(iota((width, every), 0) % rank == iota((width, every), 1) % rank)
        own_expert = iota((rows, every), 0) // ROWS == iota((rows, every), 1) // rank
        lift = jnp.zeros((every, tokens), F32)
        out_ref[:, :, half:] = jnp.zeros((experts, rank, width), BF16)
        for c in range(chunks):
            column = jnp.sum(hots[c] * wide_weight, axis=1, keepdims=True)
            placed = jnp.where(lanes, column, 0.0).astype(BF16)
            slot_weight = dot(gathered(experts), placed)
            out_ref[:, c, half:] = (slot_weight * projections[c]).astype(BF16)
            weighted = (slot_weight * latents[c]).astype(BF16)
            weighted = jnp.where(lanes, dot(spread_rows, weighted), 0.0).astype(BF16)
            weighted = jnp.where(own_expert, dot(weighted, tile), 0.0).astype(BF16)
            lift = lift + dot(weighted, hots[c].astype(BF16), ((0,), (0,)))
        lift_ref[...] = lift.astype(BF16)

    block = 512
    for n in range(half // block):
        part = dot(lift_ref[...], readout_ref[:, n * block : (n + 1) * block]).astype(BF16)
        out_ref[:, :, n * block : (n + 1) * block] = part.reshape(experts, rank, block)


def weigh(ids_t, gains_t, mask, latents, own, other, readout, experts, pairs, chunks):
    tokens, half = readout.shape
    width = latents.shape[2]
    rank = width // ROWS
    full = lambda shape: pl.BlockSpec(shape, lambda n: (0,) * len(shape))
    args = (ids_t, gains_t, mask, latents, own, other, readout)
    out = (experts, rank, half + width)
    return pl.pallas_call(
        functools.partial(weigh_body, experts, pairs, chunks),
        grid=(1,),
        in_specs=[full(x.shape) for x in args],
        out_specs=[full((1, tokens)), full(out)],
        scratch_shapes=[pltpu.VMEM((experts * rank, tokens), BF16)],
        out_shape=[jax.ShapeDtypeStruct((1, tokens), F32), jax.ShapeDtypeStruct(out, BF16)],
        compiler_params=pltpu.CompilerParams(vmem_limit_bytes=40 * 1024 * 1024),
        name="weigh_tokens",
    )(*args)


def gradients_body(groups, packed_ref, *refs):
    hid_refs, (grad_a_ref, grad_b_ref) = refs[:-2], refs[-2:]
    rank, half = grad_b_ref.shape
    block = 256
    for n in range(half // block):
        span = slice(n * block, (n + 1) * block)
        grad_b_ref[:, span] = jnp.sum(packed_ref[:, :, span].astype(F32), axis=0)
    result = jnp.zeros(grad_a_ref.shape, F32)
    at = 0
    for hid_ref in hid_refs:
        rows = hid_ref.shape[0]
        count = rows // groups
        pieces = [packed_ref[:, at + c, half:] for c in range(count // ROWS)]
        at += count // ROWS
        back = dot(spread(groups, count), jnp.concatenate(pieces, axis=1))
        back = jnp.where(own_lanes(rows, rank, count), back, 0.0).astype(BF16)
        total = dot(back, hid_ref[...], ((0,), (0,)))
        for s in range(count):
            result = result + total[s * rank : (s + 1) * rank]
    grad_a_ref[...] = result


def gradients(packed, hidden, rank):
    groups = packed.shape[0]
    half = packed.shape[2] - ROWS * rank
    hidden_units = hidden[0].shape[1]
    return pl.pallas_call(
        functools.partial(gradients_body, groups),
        out_shape=[
            jax.ShapeDtypeStruct((rank, hidden_units), F32),
            jax.ShapeDtypeStruct((rank, half), F32),
        ],
        compiler_params=pltpu.CompilerParams(vmem_limit_bytes=40 * 1024 * 1024),
        name="adapter_gradients",
    )(packed, *hidden)


def swap(payload):
    return lax.ppermute(payload, "narrow", [(0, 1), (1, 0)])


def moved(payload, groups, stride, step):
    if step == 0:
        return payload
    moves = []
    for i in range(groups):
        at = i // stride % LINE
        moves.append((i, i + ((at + step) % LINE - at) * stride))
    return lax.ppermute(payload, "wide", moves)


def exchange(payload):
    return lax.all_to_all(payload, "wide", split_axis=0, concat_axis=0, tiled=True)


def on_device(
    hidden_in,
    readout,
    route_ids,
    route_weights,
    forget_mask,
    gate_proj,
    up_proj,
    adapter_a,
    adapter_b,
):
    groups = lax.axis_size("wide")
    pairs = lax.axis_size("narrow")
    tokens, picks = route_ids.shape
    features = hidden_in.shape[1]
    half = features // pairs
    rank = adapter_a.shape[1]
    chunks = sum(PARTS) // ROWS
    side = lax.axis_index("narrow")
    core = side.reshape(1).astype(jnp.int32)

    wide = lax.axis_index("wide")
    place = jnp.stack([wide // LINE**2, wide // LINE % LINE, wide % LINE]).astype(jnp.int32)

    ids_t, gains_t = route_ids.T, route_weights.T
    own_b = lax.dynamic_slice_in_dim(adapter_b[0], side * half, half, 1)
    own_readout = lax.dynamic_slice_in_dim(readout, side * half, half, 1)

    sent = dispatch(core, ids_t, hidden_in, groups)
    x = exchange(sent[0].reshape(groups, PARTS[0], half)).reshape(groups * PARTS[0], half)
    y = exchange(sent[1].reshape(groups, PARTS[1], half)).reshape(groups * PARTS[1], half)
    acts, sums = experts_forward(
        core, x, swap(x), gate_proj, up_proj, adapter_a, [], groups, pairs, False
    )
    adapters = [moved(own_b, groups, LINE, step) for step in range(LINE)]
    acts, adapters = lax.optimization_barrier((acts, adapters))
    adapters = jnp.concatenate(adapters, axis=0)
    y, acts, adapters, own_readout = lax.optimization_barrier((y, acts, adapters, own_readout))
    adapters = [moved(adapters, groups, LINE**2, step) for step in range(LINE)]
    readouts = [moved(own_readout, groups, 1, step) for step in range(LINE)]
    last_acts, latents = experts_forward(
        core, y, swap(y), gate_proj, up_proj, adapter_a, [sums], groups, pairs, True
    )
    hidden = [acts, last_acts]
    pieces = project(readouts, adapters)
    pieces = [moved(piece, groups, 1, -step) for step, piece in enumerate(pieces)]
    projections = pick(place, ids_t, pieces, groups, chunks)
    home_latents = lax.all_to_all(
        latents, ("wide", "narrow"), split_axis=0, concat_axis=0, tiled=True
    )
    log_ratio, packed = weigh(
        ids_t,
        gains_t,
        forget_mask.reshape(1, tokens),
        home_latents,
        projections,
        swap(projections),
        own_readout,
        groups,
        pairs,
        chunks,
    )
    grad_a, part_b = gradients(exchange(packed), hidden, rank)
    other_b = swap(part_b)
    grad_b = jnp.where(
        side == 0,
        jnp.concatenate([part_b, other_b], axis=1),
        jnp.concatenate([other_b, part_b], axis=1),
    )
    return (log_ratio.reshape(tokens), grad_a[None], grad_b[None])


def solution(mesh):
    return jax.shard_map(
        on_device,
        mesh=mesh,
        in_specs=(
            P("wide", None),
            P("wide", None),
            P("wide", None),
            P("wide", None),
            P("wide"),
            P("wide", None, "narrow"),
            P("wide", None, "narrow"),
            P("wide", None, "narrow"),
            P("wide", None, None),
        ),
        out_specs=(P("wide"), P("wide", None, "narrow"), P("wide", None, None)),
        check_vma=False,
    )
```

```python
import functools

import jax
import jax.numpy as jnp
from jax import lax
from jax.experimental import pallas as pl
from jax.experimental.pallas import tpu as pltpu
from jax.sharding import PartitionSpec as P

F32 = jnp.float32
BF16 = jnp.bfloat16
ROWS = 8
LINE = 4
PARTS = (16, 8)


def iota(shape, dim):
    return lax.broadcasted_iota(jnp.int32, shape, dim)


def ones_where(condition, dtype=BF16):
    return jnp.where(condition, 1.0, 0.0).astype(dtype)


def dot(a, b, dims=((1,), (0,)), precision=None):
    return lax.dot_general(a, b, (dims, ((), ())), precision=precision, preferred_element_type=F32)


def slot_of_token(ids_t, expert):
    tokens = ids_t.shape[1]
    match = matched(ids_t, jnp.ones(ids_t.shape, F32), expert)
    before = ones_where(iota((tokens, tokens), 0) < iota((tokens, tokens), 1))
    rank = dot(match.astype(BF16), before)
    return jnp.where(match > 0.0, rank, -1.0)


def matched(ids_t, values_t, expert):
    result = jnp.zeros(expert.shape, F32)
    for k in range(ids_t.shape[0]):
        result = result + jnp.where(ids_t[k : k + 1, :] == expert, values_t[k : k + 1, :], 0.0)
    return result


def spread(groups, slots=ROWS):
    shape = (groups * slots, groups)
    return ones_where(iota(shape, 0) // slots == iota(shape, 1))


def gathered(groups):
    shape = (groups, groups * ROWS)
    return ones_where(iota(shape, 1) // ROWS == iota(shape, 0))


def full(shape):
    return pl.BlockSpec(shape, lambda *_: (0,) * len(shape))


def own_lanes(rows, rank, slots=ROWS):
    shape = (rows, slots * rank)
    return iota(shape, 0) % slots == iota(shape, 1) // rank


def one_hot_slots(slots, first, count=ROWS):
    rows = slots.shape[0] * count
    wide = dot(spread(slots.shape[0], count), slots.astype(BF16))
    wanted = (iota((rows, slots.shape[1]), 0) % count + first).astype(F32)
    return jnp.where(wide == wanted, 1.0, 0.0)


def dispatch_body(experts, core_ref, ids_ref, rows_ref, *refs):
    out_refs, hot_refs = refs[: len(PARTS)], refs[len(PARTS) :]

    @pl.when(pl.program_id(0) == 0)
    def _():
        expert = iota((experts, ids_ref.shape[1]), 0).astype(F32)
        slots = slot_of_token(ids_ref[...].astype(F32), expert)
        first = 0
        for hot_ref, count in zip(hot_refs, PARTS):
            hot_ref[...] = one_hot_slots(slots, first, count).astype(BF16)
            first += count

    rows = rows_ref[...]
    for out_ref, hot_ref in zip(out_refs, hot_refs):
        out_ref[...] = dot(hot_ref[...], rows).astype(BF16)


def dispatch(core, ids_t, rows, experts):
    tokens, features = rows.shape
    half = features // 2
    block = min(512, half)
    steps = half // block
    sizes = [experts * count for count in PARTS]
    return pl.pallas_call(
        functools.partial(dispatch_body, experts),
        grid_spec=pltpu.PrefetchScalarGridSpec(
            num_scalar_prefetch=1,
            grid=(steps,),
            in_specs=[
                pl.BlockSpec(ids_t.shape, lambda n, c: (0, 0)),
                pl.BlockSpec((tokens, block), lambda n, c: (0, c[0] * steps + n)),
            ],
            out_specs=[pl.BlockSpec((size, block), lambda n, c: (0, n)) for size in sizes],
            scratch_shapes=[pltpu.VMEM((size, tokens), BF16) for size in sizes],
        ),
        out_shape=[jax.ShapeDtypeStruct((size, half), BF16) for size in sizes],
        cost_estimate=pl.CostEstimate(
            flops=2 * sum(sizes) * tokens * half,
            bytes_accessed=2 * sum(sizes) * half,
            transcendentals=0,
        ),
        compiler_params=pltpu.CompilerParams(vmem_limit_bytes=24 * 1024 * 1024),
        name="dispatch_rows",
    )(core, ids_t, rows)


def experts_body(groups, count, steps, last, core_ref, own_ref, other_ref, go_ref, gx_ref, uo_ref, ux_ref, a_ref, *refs):
    before_refs, (hid_ref, lat_ref, acc_ref) = refs[:-3], refs[-3:]
    n = pl.program_id(0)
    own, other = own_ref[...], other_ref[...]
    gate = dot(own, go_ref[0]) + dot(other, gx_ref[0])
    up = dot(own, uo_ref[0]) + dot(other, ux_ref[0])
    hidden = (gate / (1.0 + jnp.exp(-gate)) * up).astype(BF16)
    hid_ref[...] = hidden
    rank = a_ref.shape[1]
    tiled = jnp.concatenate([a_ref[0]] * count, axis=0)
    part = dot(hidden, tiled, ((1,), (1,)))

    @pl.when(n == 0)
    def _():
        acc_ref[...] = part

    @pl.when(n > 0)
    def _():
        acc_ref[...] = acc_ref[...] + part

    @pl.when(n == steps - 1)
    def _():
        rows = groups * count
        mine = jnp.where(own_lanes(rows, rank, count), acc_ref[...], 0.0).astype(BF16)
        width = ROWS * rank
        shape = (groups // LINE, rows)
        for step in range(LINE):
            block = lax.rem(core_ref[1] + LINE - step, LINE)
            pick = ones_where(iota(shape, 1) // count == iota(shape, 0) * LINE + block)
            now = dot(pick, mine).astype(BF16)
            if last:
                at = step * LINE
                for piece in [ref[step] for ref in before_refs] + [now]:
                    for c in range(piece.shape[1] // width):
                        lat_ref[:, at, :] = piece[:, c * width : (c + 1) * width]
                        at += 1
                for c in range(at, (step + 1) * LINE):
                    lat_ref[:, c, :] = jnp.zeros((groups // LINE, width), BF16)
            else:
                lat_ref[step] = now


def experts_forward(core, own, other, gate, up, adapter_a, before, groups, last):
    rows, half = own.shape
    count = rows // groups
    hidden_units = gate.shape[2]
    rank = adapter_a.shape[1]
    block = min(256, hidden_units)
    steps = hidden_units // block
    width = count * rank
    mine = pl.BlockSpec((1, half, block), lambda n, c: (0, c[0], n))
    theirs = pl.BlockSpec((1, half, block), lambda n, c: (0, 1 - c[0], n))
    whole = pl.BlockSpec((rows, half), lambda n, c: (0, 0))
    in_specs = [whole, whole, mine, theirs, mine, theirs, pl.BlockSpec((1, rank, block), lambda n, c: (0, 0, n))]
    in_specs += [full(x.shape) for x in before]
    lines = groups // LINE
    out = (lines, LINE * LINE, ROWS * rank) if last else (LINE, lines, width)
    return pl.pallas_call(
        functools.partial(experts_body, groups, count, steps, last),
        grid_spec=pltpu.PrefetchScalarGridSpec(
            num_scalar_prefetch=1,
            grid=(steps,),
            in_specs=in_specs,
            out_specs=[
                pl.BlockSpec((rows, block), lambda n, c: (0, n)),
                full(out),
            ],
            scratch_shapes=[pltpu.VMEM((rows, width), F32)],
        ),
        out_shape=[
            jax.ShapeDtypeStruct((rows, hidden_units), BF16),
            jax.ShapeDtypeStruct(out, BF16),
        ],
        cost_estimate=pl.CostEstimate(
            flops=8 * rows * half * hidden_units,
            bytes_accessed=8 * half * hidden_units + 4 * rows * half,
            transcendentals=rows * hidden_units,
        ),
        compiler_params=pltpu.CompilerParams(vmem_limit_bytes=48 * 1024 * 1024),
        name="experts_forward",
    )(core, own, other, gate, gate, up, up, adapter_a, *before)


def project_body(tokens, *refs):
    readout_refs, adapter_refs, out_ref = refs[:LINE], refs[LINE : 2 * LINE], refs[2 * LINE]
    adapters = jnp.concatenate([ref[...] for ref in adapter_refs], axis=0)
    for step, ref in enumerate(readout_refs):
        out_ref[step * tokens : (step + 1) * tokens, :] = dot(ref[:tokens, :], adapters, ((1,), (1,)))


def project(readouts, adapters, tokens):
    half = readouts[0].shape[1]
    width = LINE * adapters[0].shape[0]
    return pl.pallas_call(
        functools.partial(project_body, tokens),
        out_shape=jax.ShapeDtypeStruct((LINE * tokens, width), F32),
        cost_estimate=pl.CostEstimate(
            flops=2 * LINE * tokens * width * half,
            bytes_accessed=2 * half * (LINE * tokens + width),
            transcendentals=0,
        ),
        compiler_params=pltpu.CompilerParams(vmem_limit_bytes=24 * 1024 * 1024),
        name="project_readout",
    )(*readouts, *adapters)


def pick_body(tokens, chunks, place_ref, own_ref, other_ref, *refs):
    info_refs, (picked_ref, hot_ref, gain_ref) = refs[:LINE], refs[LINE:]
    every = own_ref.shape[1]
    part = LINE * LINE
    rank = every // part
    rows, width = part * ROWS, ROWS * rank
    lanes = own_lanes(rows, rank)
    shape = (rows, every)
    line = iota(shape, 0) // ROWS
    back = iota(shape, 1) // rank
    row_y, row_x = line // LINE, line % LINE
    col_y = (place_ref[2] + LINE - back // LINE) % LINE
    col_x = (place_ref[3] + LINE - back % LINE) % LINE
    own_expert = (row_y == col_y) & (row_x == col_x)
    fold = ones_where(iota((every, width), 0) % rank == iota((every, width), 1) % rank)
    expert = (iota((part, tokens), 0) * LINE + place_ref[1]).astype(F32)
    for step, info_ref in enumerate(info_refs):
        ids_t = info_ref[:, :tokens].astype(F32)
        gains_t = info_ref[:, tokens : 2 * tokens].astype(F32)
        slots = slot_of_token(ids_t, expert)
        gains = dot(spread(part), matched(ids_t, gains_t, expert).astype(BF16))
        span = slice(step * tokens, (step + 1) * tokens)
        projection = (own_ref[span, :] + other_ref[span, :]).astype(BF16)
        for c in range(chunks):
            hot = one_hot_slots(slots, c * ROWS)
            at = step * chunks + c
            hot_ref[at * rows : (at + 1) * rows, :] = hot.astype(BF16)
            gain_ref[at * rows : (at + 1) * rows, :] = (hot * gains).astype(BF16)
            picked = jnp.where(own_expert, dot(hot.astype(BF16), projection), 0.0).astype(BF16)
            placed = jnp.where(lanes, dot(picked, fold), 0.0).astype(BF16)
            picked_ref[at * part : (at + 1) * part, :] = dot(gathered(part), placed)


def pick(place, own, other, infos, tokens, chunks):
    part = LINE * LINE
    width = ROWS * (own.shape[1] // part)
    count = LINE * chunks * part
    outs = [
        jax.ShapeDtypeStruct((count, width), F32),
        jax.ShapeDtypeStruct((count * ROWS, tokens), BF16),
        jax.ShapeDtypeStruct((count * ROWS, tokens), BF16),
    ]
    info = pl.BlockSpec((ROWS, 3 * tokens), lambda n, c: (tokens // ROWS, 0))
    return pl.pallas_call(
        functools.partial(pick_body, tokens, chunks),
        grid_spec=pltpu.PrefetchScalarGridSpec(
            num_scalar_prefetch=1,
            grid=(1,),
            in_specs=[full(own.shape), full(other.shape)] + [info] * LINE,
            out_specs=[full(x.shape) for x in outs],
        ),
        out_shape=outs,
        compiler_params=pltpu.CompilerParams(vmem_limit_bytes=24 * 1024 * 1024),
        name="pick_projections",
    )(place, own, other, *infos)


def rate_body(chunks, own_ref, other_ref, picked_ref, gain_ref, log_ref, latent_ref):
    part, _, width = own_ref.shape
    rank = width // ROWS
    pieces = []
    for step in range(LINE):
        for c in range(chunks):
            row = step * LINE + c
            pieces.append(own_ref[:, row, :].astype(F32) + other_ref[:, row, :].astype(F32))
    latent = jnp.concatenate(pieces, axis=0).astype(BF16)
    latent_ref[...] = latent
    same = ones_where(iota((width, width), 0) // rank == iota((width, width), 1) // rank, F32)
    score = dot(latent.astype(F32) * picked_ref[...], same, precision=lax.Precision.HIGHEST)
    rows = part * ROWS
    lanes = own_lanes(rows, rank) & (iota((rows, width), 1) % rank == 0)
    tokens = gain_ref.shape[1]
    log_ref[...] = jnp.zeros(log_ref.shape, F32)
    for step in range(LINE):
        total = jnp.zeros((1, tokens), F32)
        for c in range(chunks):
            at = step * chunks + c
            wide = dot(spread(part), score[at * part : (at + 1) * part].astype(BF16))
            column = jnp.sum(jnp.where(lanes, wide, 0.0), axis=1, keepdims=True)
            gain = gain_ref[at * rows : (at + 1) * rows, :].astype(F32)
            total = total + jnp.sum(gain * column, axis=0, keepdims=True)
        log_ref[step : step + 1, :] = total


def rate(own, other, picked, gains, chunks):
    return pl.pallas_call(
        functools.partial(rate_body, chunks),
        out_shape=[
            jax.ShapeDtypeStruct((ROWS, gains.shape[1]), F32),
            jax.ShapeDtypeStruct(picked.shape, BF16),
        ],
        compiler_params=pltpu.CompilerParams(vmem_limit_bytes=24 * 1024 * 1024),
        name="rate_tokens",
    )(own, other, picked, gains)


def weigh_body(chunks, tokens, *refs):
    log_refs, readout_refs = refs[:LINE], refs[LINE : 2 * LINE]
    latent_ref, picked_ref, hot_ref, gain_ref, out_ref, pack_ref = refs[2 * LINE :]
    part, rank, _ = pack_ref.shape
    half = readout_refs[0].shape[1]
    width = latent_ref.shape[1]
    rows = part * ROWS
    every = part * rank
    lanes = own_lanes(rows, rank)
    spread_rows = spread(part)
    tile = ones_where(iota((width, every), 0) % rank == iota((width, every), 1) % rank)
    own_expert = iota((rows, every), 0) // ROWS == iota((rows, every), 1) // rank
    lifts = []
    pack_ref[:, :, half:] = jnp.zeros((part, rank, width), BF16)
    for step in range(LINE):
        total = log_refs[0][step : step + 1, :]
        for back in range(1, LINE):
            at = (step - back) % LINE
            total = total + log_refs[back][at : at + 1, :]
        if step == 0:
            out_ref[...] = total
        mask = readout_refs[step][tokens : tokens + 1, 2 * tokens : 3 * tokens].astype(F32)
        coefficient = 2.0 * mask / (1.0 + jnp.exp(-total))
        lift = jnp.zeros((every, tokens), F32)
        for c in range(chunks):
            at = step * chunks + c
            span = slice(at * rows, (at + 1) * rows)
            weight = (gain_ref[span, :].astype(F32) * coefficient).astype(BF16).astype(F32)
            column = jnp.sum(weight, axis=1, keepdims=True)
            placed = jnp.where(lanes, column, 0.0).astype(BF16)
            weight = dot(gathered(part), placed)
            few = slice(at * part, (at + 1) * part)
            pack_ref[:, step * LINE + c, half:] = (weight * picked_ref[few, :]).astype(BF16)
            scaled = (weight * latent_ref[few, :].astype(F32)).astype(BF16)
            scaled = jnp.where(lanes, dot(spread_rows, scaled), 0.0).astype(BF16)
            scaled = jnp.where(own_expert, dot(scaled, tile), 0.0).astype(BF16)
            lift = lift + dot(scaled, hot_ref[span, :], ((0,), (0,)))
        lifts.append(lift.astype(BF16))
    lift = jnp.concatenate(lifts, axis=1)
    block = 512
    for n in range(half // block):
        span = slice(n * block, (n + 1) * block)
        rows_in = jnp.concatenate([ref[:tokens, span] for ref in readout_refs], axis=0)
        pack_ref[:, :, span] = dot(lift, rows_in).astype(BF16).reshape(part, rank, block)


def weigh(logs, readouts, latents, picked, hots, gains, rank, tokens, chunks):
    part = LINE * LINE
    half = readouts[0].shape[1]
    return pl.pallas_call(
        functools.partial(weigh_body, chunks, tokens),
        out_shape=[
            jax.ShapeDtypeStruct((1, tokens), F32),
            jax.ShapeDtypeStruct((part, rank, half + latents.shape[1]), BF16),
        ],
        compiler_params=pltpu.CompilerParams(vmem_limit_bytes=32 * 1024 * 1024),
        name="weigh_tokens",
    )(*logs, *readouts, latents, picked, hots, gains)


def gradients_body(groups, chunks, place_ref, packed_ref, *refs):
    hid_refs, (grad_a_ref, grad_b_ref) = refs[:-2], refs[-2:]
    rank, half = grad_b_ref.shape
    part = packed_ref.shape[0]
    block = 256
    for n in range(half // block):
        span = slice(n * block, (n + 1) * block)
        grad_b_ref[:, span] = jnp.sum(packed_ref[:, :, span].astype(F32), axis=0)
    result = jnp.zeros(grad_a_ref.shape, F32)
    at = 0
    for hid_ref in hid_refs:
        rows = hid_ref.shape[0]
        count = rows // groups
        stacks = []
        for c in range(count // ROWS):
            stack = [packed_ref[:, step * LINE + at + c, half:] for step in range(LINE)]
            stacks.append(jnp.concatenate(stack, axis=0))
        at += count // ROWS
        shape = (rows, LINE * part)
        group, col = iota(shape, 0) // count, iota(shape, 1)
        block_of = (place_ref[1] + LINE - col // part) % LINE
        pick = ones_where(group == (col % part) * LINE + block_of)
        back = dot(pick, jnp.concatenate(stacks, axis=1))
        back = jnp.where(own_lanes(rows, rank, count), back, 0.0).astype(BF16)
        total = dot(back, hid_ref[...], ((0,), (0,)))
        for s in range(count):
            result = result + total[s * rank : (s + 1) * rank]
    grad_a_ref[...] = result


def gradients(place, packed, hidden, groups, chunks):
    rank = packed.shape[1]
    half = packed.shape[2] - ROWS * rank
    hidden_units = hidden[0].shape[1]
    args = (packed, *hidden)
    outs = [
        jax.ShapeDtypeStruct((rank, hidden_units), F32),
        jax.ShapeDtypeStruct((rank, half), F32),
    ]
    return pl.pallas_call(
        functools.partial(gradients_body, groups, chunks),
        grid_spec=pltpu.PrefetchScalarGridSpec(
            num_scalar_prefetch=1,
            grid=(1,),
            in_specs=[full(x.shape) for x in args],
            out_specs=[full(x.shape) for x in outs],
        ),
        out_shape=outs,
        compiler_params=pltpu.CompilerParams(vmem_limit_bytes=32 * 1024 * 1024),
        name="adapter_gradients",
    )(place, *args)


def swap(payload):
    return lax.ppermute(payload, "narrow", [(0, 1), (1, 0)])


def moved(payload, groups, stride, step):
    if step == 0:
        return payload
    moves = []
    for i in range(groups):
        at = i // stride % LINE
        moves.append((i, i + ((at + step) % LINE - at) * stride))
    return lax.ppermute(payload, "wide", moves)


def exchange(payload, among=None):
    return lax.all_to_all(
        payload, "wide", split_axis=0, concat_axis=0, tiled=True, axis_index_groups=among
    )


def on_device(
    hidden_in,
    readout,
    route_ids,
    route_weights,
    forget_mask,
    gate_proj,
    up_proj,
    adapter_a,
    adapter_b,
):
    groups = lax.axis_size("wide")
    pairs = lax.axis_size("narrow")
    tokens, picks = route_ids.shape
    features = hidden_in.shape[1]
    half = features // pairs
    rank = adapter_a.shape[1]
    chunks = sum(PARTS) // ROWS
    side = lax.axis_index("narrow")
    wide = lax.axis_index("wide")
    place = [side, wide % LINE, wide // LINE**2, wide // LINE % LINE]
    place = jnp.stack(place).astype(jnp.int32)
    planes = [list(range(z, groups, LINE)) for z in range(LINE)]

    ids_t, gains_t = route_ids.T, route_weights.T
    own_b = lax.dynamic_slice_in_dim(adapter_b[0], side * half, half, 1)
    mask = jnp.broadcast_to(forget_mask.astype(BF16), (ROWS, tokens))
    info = jnp.concatenate([ids_t.astype(BF16), gains_t, mask], axis=1)
    info = jnp.pad(info, ((0, 0), (0, half - 3 * tokens)))
    own_readout = lax.dynamic_slice_in_dim(readout, side * half, half, 1)
    own_readout = jnp.concatenate([own_readout, info], axis=0)

    sent = dispatch(place, ids_t, hidden_in, groups)
    x = exchange(sent[0].reshape(groups, PARTS[0], half)).reshape(groups * PARTS[0], half)
    y = exchange(sent[1].reshape(groups, PARTS[1], half)).reshape(groups * PARTS[1], half)
    acts, sums = experts_forward(
        place, x, swap(x), gate_proj, up_proj, adapter_a, [], groups, False
    )
    adapters = [moved(own_b, groups, LINE, step) for step in range(LINE)]
    acts, adapters = lax.optimization_barrier((acts, adapters))
    adapters = jnp.concatenate(adapters, axis=0)
    y, acts, adapters, own_readout = lax.optimization_barrier((y, acts, adapters, own_readout))
    adapters = [moved(adapters, groups, LINE**2, step) for step in range(LINE)]
    readouts = [moved(own_readout, groups, 1, step) for step in range(LINE)]
    last_acts, latents = experts_forward(
        place, y, swap(y), gate_proj, up_proj, adapter_a, [sums], groups, True
    )
    last_acts, adapters, readouts = lax.optimization_barrier((last_acts, adapters, readouts))
    hidden = [acts, last_acts]
    projections = project(readouts, adapters, tokens)
    picked, hots, gains = pick(place, projections, swap(projections), readouts, tokens, chunks)
    latents, picked = lax.optimization_barrier((exchange(latents, planes), picked))
    log_part, latents = rate(latents, swap(latents), picked, gains, chunks)
    logs = [moved(log_part, groups, 1, step) for step in range(LINE)]
    log_ratio, packed = weigh(logs, readouts, latents, picked, hots, gains, rank, tokens, chunks)
    grad_a, part_b = gradients(place, exchange(packed, planes), hidden, groups, chunks)
    other_b = swap(part_b)
    grad_b = jnp.where(
        side == 0,
        jnp.concatenate([part_b, other_b], axis=1),
        jnp.concatenate([other_b, part_b], axis=1),
    )
    return (log_ratio.reshape(tokens), grad_a[None], grad_b[None])


def solution(mesh):
    return jax.shard_map(
        on_device,
        mesh=mesh,
        in_specs=(
            P("wide", None),
            P("wide", None),
            P("wide", None),
            P("wide", None),
            P("wide"),
            P("wide", None, "narrow"),
            P("wide", None, "narrow"),
            P("wide", None, "narrow"),
            P("wide", None, None),
        ),
        out_specs=(P("wide"), P("wide", None, "narrow"), P("wide", None, None)),
        check_vma=False,
    )
```

```python
import functools

import jax
import jax.numpy as jnp
from jax import lax
from jax.experimental import pallas as pl
from jax.experimental.pallas import tpu as pltpu
from jax.sharding import PartitionSpec as P

F32 = jnp.float32
BF16 = jnp.bfloat16
ROWS = 8
LINE = 4
PARTS = (16, 8)


def iota(shape, dim):
    return lax.broadcasted_iota(jnp.int32, shape, dim)


def ones_where(condition, dtype=BF16):
    return jnp.where(condition, 1.0, 0.0).astype(dtype)


def dot(a, b, dims=((1,), (0,)), precision=None):
    return lax.dot_general(a, b, (dims, ((), ())), precision=precision, preferred_element_type=F32)


def slot_of_token(ids_t, expert):
    tokens = ids_t.shape[1]
    match = matched(ids_t, jnp.ones(ids_t.shape, F32), expert)
    before = ones_where(iota((tokens, tokens), 0) < iota((tokens, tokens), 1))
    rank = dot(match.astype(BF16), before)
    return jnp.where(match > 0.0, rank, -1.0)


def matched(ids_t, values_t, expert):
    result = jnp.zeros(expert.shape, F32)
    for k in range(ids_t.shape[0]):
        result = result + jnp.where(ids_t[k : k + 1, :] == expert, values_t[k : k + 1, :], 0.0)
    return result


def spread(groups, slots=ROWS):
    shape = (groups * slots, groups)
    return ones_where(iota(shape, 0) // slots == iota(shape, 1))


def gathered(groups):
    shape = (groups, groups * ROWS)
    return ones_where(iota(shape, 1) // ROWS == iota(shape, 0))


def full(shape):
    return pl.BlockSpec(shape, lambda *_: (0,) * len(shape))


def own_lanes(rows, rank, slots=ROWS):
    shape = (rows, slots * rank)
    return iota(shape, 0) % slots == iota(shape, 1) // rank


def one_hot_slots(slots, first, count=ROWS):
    rows = slots.shape[0] * count
    wide = dot(spread(slots.shape[0], count), slots.astype(BF16))
    wanted = (iota((rows, slots.shape[1]), 0) % count + first).astype(F32)
    return jnp.where(wide == wanted, 1.0, 0.0)


def dispatch_body(experts, core_ref, ids_ref, rows_ref, *refs):
    out_refs, hot_refs = refs[: len(PARTS)], refs[len(PARTS) :]

    @pl.when(pl.program_id(0) == 0)
    def _():
        expert = iota((experts, ids_ref.shape[1]), 0).astype(F32)
        slots = slot_of_token(ids_ref[...].astype(F32), expert)
        first = 0
        for hot_ref, count in zip(hot_refs, PARTS):
            hot_ref[...] = one_hot_slots(slots, first, count).astype(BF16)
            first += count

    rows = rows_ref[...]
    for out_ref, hot_ref in zip(out_refs, hot_refs):
        out_ref[...] = dot(hot_ref[...], rows).astype(BF16)


def dispatch(core, ids_t, rows, experts):
    tokens, features = rows.shape
    half = features // 2
    block = min(512, half)
    steps = half // block
    sizes = [experts * count for count in PARTS]
    return pl.pallas_call(
        functools.partial(dispatch_body, experts),
        grid_spec=pltpu.PrefetchScalarGridSpec(
            num_scalar_prefetch=1,
            grid=(steps,),
            in_specs=[
                pl.BlockSpec(ids_t.shape, lambda n, c: (0, 0)),
                pl.BlockSpec((tokens, block), lambda n, c: (0, c[0] * steps + n)),
            ],
            out_specs=[pl.BlockSpec((size, block), lambda n, c: (0, n)) for size in sizes],
            scratch_shapes=[pltpu.VMEM((size, tokens), BF16) for size in sizes],
        ),
        out_shape=[jax.ShapeDtypeStruct((size, half), BF16) for size in sizes],
        cost_estimate=pl.CostEstimate(
            flops=2 * sum(sizes) * tokens * half,
            bytes_accessed=2 * sum(sizes) * half,
            transcendentals=0,
        ),
        compiler_params=pltpu.CompilerParams(vmem_limit_bytes=20 * 1024 * 1024),
        name="dispatch_rows",
    )(core, ids_t, rows)


def experts_body(groups, count, steps, last, core_ref, own_ref, other_ref, go_ref, gx_ref, uo_ref, ux_ref, a_ref, *refs):
    before_refs, (hid_ref, lat_ref, acc_ref) = refs[:-3], refs[-3:]
    n = pl.program_id(0)
    own, other = own_ref[...], other_ref[...]
    gate = dot(own, go_ref[0]) + dot(other, gx_ref[0])
    up = dot(own, uo_ref[0]) + dot(other, ux_ref[0])
    hidden = (gate / (1.0 + jnp.exp(-gate)) * up).astype(BF16)
    hid_ref[...] = hidden
    rank = a_ref.shape[1]
    tiled = jnp.concatenate([a_ref[0]] * count, axis=0)
    part = dot(hidden, tiled, ((1,), (1,)))

    @pl.when(n == 0)
    def _():
        acc_ref[...] = part

    @pl.when(n > 0)
    def _():
        acc_ref[...] = acc_ref[...] + part

    @pl.when(n == steps - 1)
    def _():
        rows = groups * count
        mine = jnp.where(own_lanes(rows, rank, count), acc_ref[...], 0.0).astype(BF16)
        width = ROWS * rank
        shape = (groups // LINE, rows)
        for step in range(LINE):
            block = lax.rem(core_ref[1] + LINE - step, LINE)
            pick = ones_where(iota(shape, 1) // count == iota(shape, 0) * LINE + block)
            now = dot(pick, mine).astype(BF16)
            if last:
                at = step * LINE
                for piece in [ref[step] for ref in before_refs] + [now]:
                    for c in range(piece.shape[1] // width):
                        lat_ref[:, at, :] = piece[:, c * width : (c + 1) * width]
                        at += 1
                for c in range(at, (step + 1) * LINE):
                    lat_ref[:, c, :] = jnp.zeros((groups // LINE, width), BF16)
            else:
                lat_ref[step] = now


def experts_forward(core, own, other, gate, up, adapter_a, before, groups, last):
    rows, half = own.shape
    count = rows // groups
    hidden_units = gate.shape[2]
    rank = adapter_a.shape[1]
    block = min(256, hidden_units)
    steps = hidden_units // block
    width = count * rank
    mine = pl.BlockSpec((1, half, block), lambda n, c: (0, c[0], n))
    theirs = pl.BlockSpec((1, half, block), lambda n, c: (0, 1 - c[0], n))
    whole = pl.BlockSpec((rows, half), lambda n, c: (0, 0))
    in_specs = [whole, whole, mine, theirs, mine, theirs, pl.BlockSpec((1, rank, block), lambda n, c: (0, 0, n))]
    in_specs += [full(x.shape) for x in before]
    lines = groups // LINE
    out = (lines, LINE * LINE, ROWS * rank) if last else (LINE, lines, width)
    return pl.pallas_call(
        functools.partial(experts_body, groups, count, steps, last),
        grid_spec=pltpu.PrefetchScalarGridSpec(
            num_scalar_prefetch=1,
            grid=(steps,),
            in_specs=in_specs,
            out_specs=[
                pl.BlockSpec((rows, block), lambda n, c: (0, n)),
                full(out),
            ],
            scratch_shapes=[pltpu.VMEM((rows, width), F32)],
        ),
        out_shape=[
            jax.ShapeDtypeStruct((rows, hidden_units), BF16),
            jax.ShapeDtypeStruct(out, BF16),
        ],
        cost_estimate=pl.CostEstimate(
            flops=8 * rows * half * hidden_units,
            bytes_accessed=8 * half * hidden_units + 4 * rows * half,
            transcendentals=rows * hidden_units,
        ),
        compiler_params=pltpu.CompilerParams(vmem_limit_bytes=48 * 1024 * 1024),
        name="experts_forward",
    )(core, own, other, gate, gate, up, up, adapter_a, *before)


def project_body(tokens, *refs):
    readout_refs, adapter_refs, out_ref = refs[:LINE], refs[LINE : 2 * LINE], refs[2 * LINE]
    adapters = jnp.concatenate([ref[...] for ref in adapter_refs], axis=0)
    for step, ref in enumerate(readout_refs):
        out_ref[step * tokens : (step + 1) * tokens, :] = dot(ref[:tokens, :], adapters, ((1,), (1,)))


def project(readouts, adapters, tokens):
    half = readouts[0].shape[1]
    width = LINE * adapters[0].shape[0]
    return pl.pallas_call(
        functools.partial(project_body, tokens),
        out_shape=jax.ShapeDtypeStruct((LINE * tokens, width), F32),
        cost_estimate=pl.CostEstimate(
            flops=2 * LINE * tokens * width * half,
            bytes_accessed=2 * half * (LINE * tokens + width),
            transcendentals=0,
        ),
        compiler_params=pltpu.CompilerParams(vmem_limit_bytes=16 * 1024 * 1024),
        name="project_readout",
    )(*readouts, *adapters)


def pick_body(tokens, chunks, place_ref, own_ref, other_ref, *refs):
    info_refs, (picked_ref, gain_ref) = refs[:LINE], refs[LINE:]
    every = own_ref.shape[1]
    part = LINE * LINE
    rank = every // part
    rows, width = part * ROWS, ROWS * rank
    lanes = own_lanes(rows, rank)
    shape = (rows, every)
    line = iota(shape, 0) // ROWS
    back = iota(shape, 1) // rank
    row_y, row_x = line // LINE, line % LINE
    col_y = (place_ref[2] + LINE - back // LINE) % LINE
    col_x = (place_ref[3] + LINE - back % LINE) % LINE
    own_expert = (row_y == col_y) & (row_x == col_x)
    fold = ones_where(iota((every, width), 0) % rank == iota((every, width), 1) % rank)
    expert = (iota((part, tokens), 0) * LINE + place_ref[1]).astype(F32)
    for step, info_ref in enumerate(info_refs):
        ids_t = info_ref[:, :tokens].astype(F32)
        gains_t = info_ref[:, tokens : 2 * tokens].astype(F32)
        slots = slot_of_token(ids_t, expert)
        gains = dot(spread(part), matched(ids_t, gains_t, expert).astype(BF16))
        span = slice(step * tokens, (step + 1) * tokens)
        projection = (own_ref[span, :] + other_ref[span, :]).astype(BF16)
        for c in range(chunks):
            hot = one_hot_slots(slots, c * ROWS)
            at = step * chunks + c
            gain_ref[at * rows : (at + 1) * rows, :] = (hot * gains).astype(BF16)
            picked = jnp.where(own_expert, dot(hot.astype(BF16), projection), 0.0).astype(BF16)
            placed = jnp.where(lanes, dot(picked, fold), 0.0).astype(BF16)
            picked_ref[at * part : (at + 1) * part, :] = dot(gathered(part), placed)


def pick(place, own, other, infos, tokens, chunks):
    part = LINE * LINE
    width = ROWS * (own.shape[1] // part)
    count = LINE * chunks * part
    outs = [
        jax.ShapeDtypeStruct((count, width), F32),
        jax.ShapeDtypeStruct((count * ROWS, tokens), BF16),
    ]
    info = pl.BlockSpec((ROWS, 3 * tokens), lambda n, c: (tokens // ROWS, 0))
    return pl.pallas_call(
        functools.partial(pick_body, tokens, chunks),
        grid_spec=pltpu.PrefetchScalarGridSpec(
            num_scalar_prefetch=1,
            grid=(1,),
            in_specs=[full(own.shape), full(other.shape)] + [info] * LINE,
            out_specs=[full(x.shape) for x in outs],
        ),
        out_shape=outs,
        compiler_params=pltpu.CompilerParams(vmem_limit_bytes=16 * 1024 * 1024),
        name="pick_projections",
    )(place, own, other, *infos)


def rate_body(chunks, own_ref, other_ref, picked_ref, gain_ref, log_ref, latent_ref):
    part, _, width = own_ref.shape
    rank = width // ROWS
    pieces = []
    for step in range(LINE):
        for c in range(chunks):
            row = step * LINE + c
            pieces.append(own_ref[:, row, :].astype(F32) + other_ref[:, row, :].astype(F32))
    latent = jnp.concatenate(pieces, axis=0).astype(BF16)
    latent_ref[...] = latent
    same = ones_where(iota((width, width), 0) // rank == iota((width, width), 1) // rank, F32)
    score = dot(latent.astype(F32) * picked_ref[...], same, precision=lax.Precision.HIGHEST)
    rows = part * ROWS
    lanes = own_lanes(rows, rank) & (iota((rows, width), 1) % rank == 0)
    tokens = gain_ref.shape[1]
    log_ref[...] = jnp.zeros(log_ref.shape, F32)
    for step in range(LINE):
        total = jnp.zeros((1, tokens), F32)
        for c in range(chunks):
            at = step * chunks + c
            wide = dot(spread(part), score[at * part : (at + 1) * part].astype(BF16))
            column = jnp.sum(jnp.where(lanes, wide, 0.0), axis=1, keepdims=True)
            gain = gain_ref[at * rows : (at + 1) * rows, :].astype(F32)
            total = total + jnp.sum(gain * column, axis=0, keepdims=True)
        log_ref[step : step + 1, :] = total


def rate(own, other, picked, gains, chunks):
    return pl.pallas_call(
        functools.partial(rate_body, chunks),
        out_shape=[
            jax.ShapeDtypeStruct((ROWS, gains.shape[1]), F32),
            jax.ShapeDtypeStruct(picked.shape, BF16),
        ],
        compiler_params=pltpu.CompilerParams(vmem_limit_bytes=12 * 1024 * 1024),
        name="rate_tokens",
    )(own, other, picked, gains)


def weigh_body(chunks, tokens, *refs):
    log_refs, readout_refs = refs[:LINE], refs[LINE : 2 * LINE]
    latent_ref, picked_ref, gain_ref, out_ref, pack_ref = refs[2 * LINE :]
    part, rank, _ = pack_ref.shape
    half = readout_refs[0].shape[1]
    width = latent_ref.shape[1]
    rows = part * ROWS
    every = part * rank
    lanes = own_lanes(rows, rank)
    spread_rows = spread(part)
    tile = ones_where(iota((width, every), 0) % rank == iota((width, every), 1) % rank)
    own_expert = iota((rows, every), 0) // ROWS == iota((rows, every), 1) // rank
    lifts = []
    pack_ref[:, :, half:] = jnp.zeros((part, rank, width), BF16)
    for step in range(LINE):
        total = log_refs[0][step : step + 1, :]
        for back in range(1, LINE):
            at = (step - back) % LINE
            total = total + log_refs[back][at : at + 1, :]
        if step == 0:
            out_ref[...] = total
        mask = readout_refs[step][tokens : tokens + 1, 2 * tokens : 3 * tokens].astype(F32)
        coefficient = 2.0 * mask / (1.0 + jnp.exp(-total))
        lift = jnp.zeros((every, tokens), F32)
        for c in range(chunks):
            at = step * chunks + c
            span = slice(at * rows, (at + 1) * rows)
            gain = gain_ref[span, :].astype(F32)
            hot = ones_where(gain > 0.0)
            weight = (gain * coefficient).astype(BF16).astype(F32)
            column = jnp.sum(weight, axis=1, keepdims=True)
            placed = jnp.where(lanes, column, 0.0).astype(BF16)
            weight = dot(gathered(part), placed)
            few = slice(at * part, (at + 1) * part)
            pack_ref[:, step * LINE + c, half:] = (weight * picked_ref[few, :]).astype(BF16)
            scaled = (weight * latent_ref[few, :].astype(F32)).astype(BF16)
            scaled = jnp.where(lanes, dot(spread_rows, scaled), 0.0).astype(BF16)
            scaled = jnp.where(own_expert, dot(scaled, tile), 0.0).astype(BF16)
            lift = lift + dot(scaled, hot, ((0,), (0,)))
        lifts.append(lift.astype(BF16))
    lift = jnp.concatenate(lifts, axis=1)
    block = 512
    for n in range(half // block):
        span = slice(n * block, (n + 1) * block)
        rows_in = jnp.concatenate([ref[:tokens, span] for ref in readout_refs], axis=0)
        pack_ref[:, :, span] = dot(lift, rows_in).astype(BF16).reshape(part, rank, block)


def weigh(logs, readouts, latents, picked, gains, rank, tokens, chunks):
    part = LINE * LINE
    half = readouts[0].shape[1]
    return pl.pallas_call(
        functools.partial(weigh_body, chunks, tokens),
        out_shape=[
            jax.ShapeDtypeStruct((1, tokens), F32),
            jax.ShapeDtypeStruct((part, rank, half + latents.shape[1]), BF16),
        ],
        compiler_params=pltpu.CompilerParams(vmem_limit_bytes=20 * 1024 * 1024),
        name="weigh_tokens",
    )(*logs, *readouts, latents, picked, gains)


def gradients_body(groups, chunks, place_ref, packed_ref, *refs):
    hid_refs, (grad_a_ref, grad_b_ref) = refs[:-2], refs[-2:]
    rank, half = grad_b_ref.shape
    part = packed_ref.shape[0]
    block = 256
    for n in range(half // block):
        span = slice(n * block, (n + 1) * block)
        grad_b_ref[:, span] = jnp.sum(packed_ref[:, :, span].astype(F32), axis=0)
    result = jnp.zeros(grad_a_ref.shape, F32)
    at = 0
    for hid_ref in hid_refs:
        rows = hid_ref.shape[0]
        count = rows // groups
        stacks = []
        for c in range(count // ROWS):
            stack = [packed_ref[:, step * LINE + at + c, half:] for step in range(LINE)]
            stacks.append(jnp.concatenate(stack, axis=0))
        at += count // ROWS
        shape = (rows, LINE * part)
        group, col = iota(shape, 0) // count, iota(shape, 1)
        block_of = (place_ref[1] + LINE - col // part) % LINE
        pick = ones_where(group == (col % part) * LINE + block_of)
        back = dot(pick, jnp.concatenate(stacks, axis=1))
        back = jnp.where(own_lanes(rows, rank, count), back, 0.0).astype(BF16)
        total = dot(back, hid_ref[...], ((0,), (0,)))
        for s in range(count):
            result = result + total[s * rank : (s + 1) * rank]
    grad_a_ref[...] = result


def gradients(place, packed, hidden, groups, chunks):
    rank = packed.shape[1]
    half = packed.shape[2] - ROWS * rank
    hidden_units = hidden[0].shape[1]
    args = (packed, *hidden)
    outs = [
        jax.ShapeDtypeStruct((rank, hidden_units), F32),
        jax.ShapeDtypeStruct((rank, half), F32),
    ]
    return pl.pallas_call(
        functools.partial(gradients_body, groups, chunks),
        grid_spec=pltpu.PrefetchScalarGridSpec(
            num_scalar_prefetch=1,
            grid=(1,),
            in_specs=[full(x.shape) for x in args],
            out_specs=[full(x.shape) for x in outs],
        ),
        out_shape=outs,
        compiler_params=pltpu.CompilerParams(vmem_limit_bytes=20 * 1024 * 1024),
        name="adapter_gradients",
    )(place, *args)


def swap(payload):
    return lax.ppermute(payload, "narrow", [(0, 1), (1, 0)])


def moved(payload, groups, stride, step):
    if step == 0:
        return payload
    moves = []
    for i in range(groups):
        at = i // stride % LINE
        moves.append((i, i + ((at + step) % LINE - at) * stride))
    return lax.ppermute(payload, "wide", moves)


def exchange(payload, among=None):
    return lax.all_to_all(
        payload, "wide", split_axis=0, concat_axis=0, tiled=True, axis_index_groups=among
    )


def on_device(
    hidden_in,
    readout,
    route_ids,
    route_weights,
    forget_mask,
    gate_proj,
    up_proj,
    adapter_a,
    adapter_b,
):
    groups = lax.axis_size("wide")
    pairs = lax.axis_size("narrow")
    tokens, picks = route_ids.shape
    features = hidden_in.shape[1]
    half = features // pairs
    rank = adapter_a.shape[1]
    chunks = sum(PARTS) // ROWS
    side = lax.axis_index("narrow")
    wide = lax.axis_index("wide")
    place = [side, wide % LINE, wide // LINE**2, wide // LINE % LINE]
    place = jnp.stack(place).astype(jnp.int32)
    planes = [list(range(z, groups, LINE)) for z in range(LINE)]

    ids_t, gains_t = route_ids.T, route_weights.T
    own_b = lax.dynamic_slice_in_dim(adapter_b[0], side * half, half, 1)
    mask = jnp.broadcast_to(forget_mask.astype(BF16), (ROWS, tokens))
    info = jnp.concatenate([ids_t.astype(BF16), gains_t, mask], axis=1)
    info = jnp.pad(info, ((0, 0), (0, half - 3 * tokens)))
    own_readout = lax.dynamic_slice_in_dim(readout, side * half, half, 1)
    own_readout = jnp.concatenate([own_readout, info], axis=0)

    adapters = [moved(own_b, groups, LINE, step) for step in range(LINE)]
    adapters = jnp.concatenate(adapters, axis=0)
    sent = list(dispatch(place, ids_t, hidden_in, groups))
    sent[0], adapters = lax.optimization_barrier((sent[0], adapters))
    x = exchange(sent[0].reshape(groups, PARTS[0], half)).reshape(groups * PARTS[0], half)
    y = exchange(sent[1].reshape(groups, PARTS[1], half)).reshape(groups * PARTS[1], half)
    acts, sums = experts_forward(
        place, x, swap(x), gate_proj, up_proj, adapter_a, [], groups, False
    )
    adapters = [moved(adapters, groups, LINE**2, step) for step in range(LINE)]
    y, acts, adapters, own_readout = lax.optimization_barrier((y, acts, adapters, own_readout))
    readouts = [moved(own_readout, groups, 1, step) for step in range(LINE)]
    last_acts, latents = experts_forward(
        place, y, swap(y), gate_proj, up_proj, adapter_a, [sums], groups, True
    )
    last_acts, adapters, readouts = lax.optimization_barrier((last_acts, adapters, readouts))
    hidden = [acts, last_acts]
    projections = project(readouts, adapters, tokens)
    picked, gains = pick(place, projections, swap(projections), readouts, tokens, chunks)
    latents, picked = lax.optimization_barrier((exchange(latents, planes), picked))
    log_part, latents = rate(latents, swap(latents), picked, gains, chunks)
    logs = [moved(log_part, groups, 1, step) for step in range(LINE)]
    log_ratio, packed = weigh(logs, readouts, latents, picked, gains, rank, tokens, chunks)
    grad_a, part_b = gradients(place, exchange(packed, planes), hidden, groups, chunks)
    other_b = swap(part_b)
    grad_b = jnp.where(
        side == 0,
        jnp.concatenate([part_b, other_b], axis=1),
        jnp.concatenate([other_b, part_b], axis=1),
    )
    return (log_ratio.reshape(tokens), grad_a[None], grad_b[None])


def solution(mesh):
    return jax.shard_map(
        on_device,
        mesh=mesh,
        in_specs=(
            P("wide", None),
            P("wide", None),
            P("wide", None),
            P("wide", None),
            P("wide"),
            P("wide", None, "narrow"),
            P("wide", None, "narrow"),
            P("wide", None, "narrow"),
            P("wide", None, None),
        ),
        out_specs=(P("wide"), P("wide", None, "narrow"), P("wide", None, None)),
        check_vma=False,
    )
```

```python
import functools

import jax
import jax.numpy as jnp
from jax import lax
from jax.experimental import pallas as pl
from jax.experimental.pallas import tpu as pltpu
from jax.sharding import PartitionSpec as P

F32 = jnp.float32
BF16 = jnp.bfloat16
ROWS = 8
LINE = 4
PARTS = (24,)


def iota(shape, dim):
    return lax.broadcasted_iota(jnp.int32, shape, dim)


def ones_where(condition, dtype=BF16):
    return jnp.where(condition, 1.0, 0.0).astype(dtype)


def dot(a, b, dims=((1,), (0,)), precision=None):
    return lax.dot_general(a, b, (dims, ((), ())), precision=precision, preferred_element_type=F32)


def slot_of_token(ids_t, expert):
    tokens = ids_t.shape[1]
    match = matched(ids_t, jnp.ones(ids_t.shape, F32), expert)
    before = ones_where(iota((tokens, tokens), 0) < iota((tokens, tokens), 1))
    rank = dot(match.astype(BF16), before)
    return jnp.where(match > 0.0, rank, -1.0)


def matched(ids_t, values_t, expert):
    result = jnp.zeros(expert.shape, F32)
    for k in range(ids_t.shape[0]):
        result = result + jnp.where(ids_t[k : k + 1, :] == expert, values_t[k : k + 1, :], 0.0)
    return result


def spread(groups, slots=ROWS):
    shape = (groups * slots, groups)
    return ones_where(iota(shape, 0) // slots == iota(shape, 1))


def gathered(groups):
    shape = (groups, groups * ROWS)
    return ones_where(iota(shape, 1) // ROWS == iota(shape, 0))


def full(shape):
    return pl.BlockSpec(shape, lambda *_: (0,) * len(shape))


def own_lanes(rows, rank, slots=ROWS):
    shape = (rows, slots * rank)
    return iota(shape, 0) % slots == iota(shape, 1) // rank


def one_hot_slots(slots, first, count=ROWS):
    rows = slots.shape[0] * count
    wide = dot(spread(slots.shape[0], count), slots.astype(BF16))
    wanted = (iota((rows, slots.shape[1]), 0) % count + first).astype(F32)
    return jnp.where(wide == wanted, 1.0, 0.0)


def dispatch_body(experts, core_ref, ids_ref, rows_ref, *refs):
    out_refs, hot_refs = refs[: len(PARTS)], refs[len(PARTS) :]

    @pl.when(pl.program_id(0) == 0)
    def _():
        expert = iota((experts, ids_ref.shape[1]), 0).astype(F32)
        slots = slot_of_token(ids_ref[...].astype(F32), expert)
        first = 0
        for hot_ref, count in zip(hot_refs, PARTS):
            hot_ref[...] = one_hot_slots(slots, first, count).astype(BF16)
            first += count

    rows = rows_ref[...]
    for out_ref, hot_ref in zip(out_refs, hot_refs):
        out_ref[...] = dot(hot_ref[...], rows).astype(BF16)


def dispatch(core, ids_t, rows, experts):
    tokens, features = rows.shape
    half = features // 2
    block = min(512, half)
    steps = half // block
    sizes = [experts * count for count in PARTS]
    return pl.pallas_call(
        functools.partial(dispatch_body, experts),
        grid_spec=pltpu.PrefetchScalarGridSpec(
            num_scalar_prefetch=1,
            grid=(steps,),
            in_specs=[
                pl.BlockSpec(ids_t.shape, lambda n, c: (0, 0)),
                pl.BlockSpec((tokens, block), lambda n, c: (0, c[0] * steps + n)),
            ],
            out_specs=[pl.BlockSpec((size, block), lambda n, c: (0, n)) for size in sizes],
            scratch_shapes=[pltpu.VMEM((size, tokens), BF16) for size in sizes],
        ),
        out_shape=[jax.ShapeDtypeStruct((size, half), BF16) for size in sizes],
        cost_estimate=pl.CostEstimate(
            flops=2 * sum(sizes) * tokens * half,
            bytes_accessed=2 * sum(sizes) * half,
            transcendentals=0,
        ),
        compiler_params=pltpu.CompilerParams(vmem_limit_bytes=58 * 1024 * 1024),
        name="dispatch_rows",
    )(core, ids_t, rows)


def experts_body(count, steps, core_ref, own_ref, other_ref, go_ref, gx_ref, uo_ref, ux_ref, a_ref, hid_ref, lat_ref, acc_ref):
    n = pl.program_id(1)
    own, other = own_ref[...], other_ref[...]
    gate = dot(own, go_ref[0]) + dot(other, gx_ref[0])
    up = dot(own, uo_ref[0]) + dot(other, ux_ref[0])
    hidden = (gate / (1.0 + jnp.exp(-gate)) * up).astype(BF16)
    hid_ref[...] = hidden
    rank = a_ref.shape[1]
    tiled = jnp.concatenate([a_ref[0]] * count, axis=0)
    part = dot(hidden, tiled, ((1,), (1,)))

    @pl.when(n == 0)
    def _():
        acc_ref[...] = part

    @pl.when(n > 0)
    def _():
        acc_ref[...] = acc_ref[...] + part

    @pl.when(n == steps - 1)
    def _():
        rows = acc_ref.shape[0]
        mine = jnp.where(own_lanes(rows, rank, count), acc_ref[...], 0.0).astype(BF16)
        width = ROWS * rank
        lines = lat_ref.shape[0]
        shape = (lines, rows)
        for step in range(LINE):
            block = lax.rem(core_ref[1] + LINE - step, LINE)
            pick = ones_where(iota(shape, 1) // count == iota(shape, 0) * LINE + block)
            now = dot(pick, mine).astype(BF16)
            for c in range(count // ROWS):
                lat_ref[:, step * LINE + c, :] = now[:, c * width : (c + 1) * width]
            for c in range(count // ROWS, LINE):
                lat_ref[:, step * LINE + c, :] = jnp.zeros((lines, width), BF16)


def experts_forward(core, own, other, gate, up, adapter_a, groups):
    total, half = own.shape
    count = total // groups
    hidden_units = gate.shape[2]
    rank = adapter_a.shape[1]
    block = min(256, hidden_units)
    steps = hidden_units // block
    passes = 2
    rows = total // passes
    lines = groups // LINE
    mine = pl.BlockSpec((1, half, block), lambda m, n, c: (0, c[0], n))
    theirs = pl.BlockSpec((1, half, block), lambda m, n, c: (0, 1 - c[0], n))
    some = pl.BlockSpec((rows, half), lambda m, n, c: (m, 0))
    lat = (LINE * LINE, ROWS * rank)
    return pl.pallas_call(
        functools.partial(experts_body, count, steps),
        grid_spec=pltpu.PrefetchScalarGridSpec(
            num_scalar_prefetch=1,
            grid=(passes, steps),
            in_specs=[some, some, mine, theirs, mine, theirs]
            + [pl.BlockSpec((1, rank, block), lambda m, n, c: (0, 0, n))],
            out_specs=[
                pl.BlockSpec((rows, block), lambda m, n, c: (m, n)),
                pl.BlockSpec((lines // passes, *lat), lambda m, n, c: (m, 0, 0)),
            ],
            scratch_shapes=[pltpu.VMEM((rows, count * rank), F32)],
        ),
        out_shape=[
            jax.ShapeDtypeStruct((total, hidden_units), BF16),
            jax.ShapeDtypeStruct((lines, *lat), BF16),
        ],
        cost_estimate=pl.CostEstimate(
            flops=8 * total * half * hidden_units,
            bytes_accessed=8 * passes * half * hidden_units + 4 * total * half,
            transcendentals=total * hidden_units,
        ),
        compiler_params=pltpu.CompilerParams(vmem_limit_bytes=60 * 1024 * 1024),
        name="experts_forward",
    )(core, own, other, gate, gate, up, up, adapter_a)


def project_body(tokens, *refs):
    readout_refs, adapter_refs, out_ref = refs[:LINE], refs[LINE : 2 * LINE], refs[2 * LINE]
    adapters = jnp.concatenate([ref[...] for ref in adapter_refs], axis=0)
    for step, ref in enumerate(readout_refs):
        out_ref[step * tokens : (step + 1) * tokens, :] = dot(ref[:tokens, :], adapters, ((1,), (1,)))


def project(readouts, adapters, tokens):
    half = readouts[0].shape[1]
    width = LINE * adapters[0].shape[0]
    return pl.pallas_call(
        functools.partial(project_body, tokens),
        out_shape=jax.ShapeDtypeStruct((LINE * tokens, width), F32),
        cost_estimate=pl.CostEstimate(
            flops=2 * LINE * tokens * width * half,
            bytes_accessed=2 * half * (LINE * tokens + width),
            transcendentals=0,
        ),
        compiler_params=pltpu.CompilerParams(vmem_limit_bytes=16 * 1024 * 1024),
        name="project_readout",
    )(*readouts, *adapters)


def pick_body(tokens, chunks, place_ref, own_ref, other_ref, *refs):
    info_refs, (picked_ref, gain_ref) = refs[:LINE], refs[LINE:]
    every = own_ref.shape[1]
    part = LINE * LINE
    rank = every // part
    rows, width = part * ROWS, ROWS * rank
    lanes = own_lanes(rows, rank)
    shape = (rows, every)
    line = iota(shape, 0) // ROWS
    back = iota(shape, 1) // rank
    row_y, row_x = line // LINE, line % LINE
    col_y = (place_ref[2] + LINE - back // LINE) % LINE
    col_x = (place_ref[3] + LINE - back % LINE) % LINE
    own_expert = (row_y == col_y) & (row_x == col_x)
    fold = ones_where(iota((every, width), 0) % rank == iota((every, width), 1) % rank)
    expert = (iota((part, tokens), 0) * LINE + place_ref[1]).astype(F32)
    for step, info_ref in enumerate(info_refs):
        ids_t = info_ref[:, :tokens].astype(F32)
        gains_t = info_ref[:, tokens : 2 * tokens].astype(F32)
        slots = slot_of_token(ids_t, expert)
        gains = dot(spread(part), matched(ids_t, gains_t, expert).astype(BF16))
        span = slice(step * tokens, (step + 1) * tokens)
        projection = (own_ref[span, :] + other_ref[span, :]).astype(BF16)
        for c in range(chunks):
            hot = one_hot_slots(slots, c * ROWS)
            at = step * chunks + c
            gain_ref[at * rows : (at + 1) * rows, :] = (hot * gains).astype(BF16)
            picked = jnp.where(own_expert, dot(hot.astype(BF16), projection), 0.0).astype(BF16)
            placed = jnp.where(lanes, dot(picked, fold), 0.0).astype(BF16)
            picked_ref[at * part : (at + 1) * part, :] = dot(gathered(part), placed)


def pick(place, own, other, infos, tokens, chunks):
    part = LINE * LINE
    width = ROWS * (own.shape[1] // part)
    count = LINE * chunks * part
    outs = [
        jax.ShapeDtypeStruct((count, width), F32),
        jax.ShapeDtypeStruct((count * ROWS, tokens), BF16),
    ]
    info = pl.BlockSpec((ROWS, 3 * tokens), lambda n, c: (tokens // ROWS, 0))
    return pl.pallas_call(
        functools.partial(pick_body, tokens, chunks),
        grid_spec=pltpu.PrefetchScalarGridSpec(
            num_scalar_prefetch=1,
            grid=(1,),
            in_specs=[full(own.shape), full(other.shape)] + [info] * LINE,
            out_specs=[full(x.shape) for x in outs],
        ),
        out_shape=outs,
        compiler_params=pltpu.CompilerParams(vmem_limit_bytes=16 * 1024 * 1024),
        name="pick_projections",
    )(place, own, other, *infos)


def rate_body(chunks, own_ref, other_ref, picked_ref, gain_ref, log_ref, latent_ref):
    part, _, width = own_ref.shape
    rank = width // ROWS
    pieces = []
    for step in range(LINE):
        for c in range(chunks):
            row = step * LINE + c
            pieces.append(own_ref[:, row, :].astype(F32) + other_ref[:, row, :].astype(F32))
    latent = jnp.concatenate(pieces, axis=0).astype(BF16)
    latent_ref[...] = latent
    same = ones_where(iota((width, width), 0) // rank == iota((width, width), 1) // rank, F32)
    score = dot(latent.astype(F32) * picked_ref[...], same, precision=lax.Precision.HIGHEST)
    rows = part * ROWS
    lanes = own_lanes(rows, rank) & (iota((rows, width), 1) % rank == 0)
    tokens = gain_ref.shape[1]
    log_ref[...] = jnp.zeros(log_ref.shape, F32)
    for step in range(LINE):
        total = jnp.zeros((1, tokens), F32)
        for c in range(chunks):
            at = step * chunks + c
            wide = dot(spread(part), score[at * part : (at + 1) * part].astype(BF16))
            column = jnp.sum(jnp.where(lanes, wide, 0.0), axis=1, keepdims=True)
            gain = gain_ref[at * rows : (at + 1) * rows, :].astype(F32)
            total = total + jnp.sum(gain * column, axis=0, keepdims=True)
        log_ref[step : step + 1, :] = total


def rate(own, other, picked, gains, chunks):
    return pl.pallas_call(
        functools.partial(rate_body, chunks),
        out_shape=[
            jax.ShapeDtypeStruct((ROWS, gains.shape[1]), F32),
            jax.ShapeDtypeStruct(picked.shape, BF16),
        ],
        compiler_params=pltpu.CompilerParams(vmem_limit_bytes=12 * 1024 * 1024),
        name="rate_tokens",
    )(own, other, picked, gains)


def weigh_body(chunks, tokens, *refs):
    log_refs, readout_refs = refs[:LINE], refs[LINE : 2 * LINE]
    latent_ref, picked_ref, gain_ref, out_ref, pack_ref = refs[2 * LINE :]
    part, rank, _ = pack_ref.shape
    half = readout_refs[0].shape[1]
    width = latent_ref.shape[1]
    rows = part * ROWS
    every = part * rank
    lanes = own_lanes(rows, rank)
    spread_rows = spread(part)
    tile = ones_where(iota((width, every), 0) % rank == iota((width, every), 1) % rank)
    own_expert = iota((rows, every), 0) // ROWS == iota((rows, every), 1) // rank
    lifts = []
    pack_ref[:, :, half:] = jnp.zeros((part, rank, width), BF16)
    for step in range(LINE):
        total = log_refs[0][step : step + 1, :]
        for back in range(1, LINE):
            at = (step - back) % LINE
            total = total + log_refs[back][at : at + 1, :]
        if step == 0:
            out_ref[...] = total
        mask = readout_refs[step][tokens : tokens + 1, 2 * tokens : 3 * tokens].astype(F32)
        coefficient = 2.0 * mask / (1.0 + jnp.exp(-total))
        lift = jnp.zeros((every, tokens), F32)
        for c in range(chunks):
            at = step * chunks + c
            span = slice(at * rows, (at + 1) * rows)
            gain = gain_ref[span, :].astype(F32)
            hot = ones_where(gain > 0.0)
            weight = (gain * coefficient).astype(BF16).astype(F32)
            column = jnp.sum(weight, axis=1, keepdims=True)
            placed = jnp.where(lanes, column, 0.0).astype(BF16)
            weight = dot(gathered(part), placed)
            few = slice(at * part, (at + 1) * part)
            pack_ref[:, step * LINE + c, half:] = (weight * picked_ref[few, :]).astype(BF16)
            scaled = (weight * latent_ref[few, :].astype(F32)).astype(BF16)
            scaled = jnp.where(lanes, dot(spread_rows, scaled), 0.0).astype(BF16)
            scaled = jnp.where(own_expert, dot(scaled, tile), 0.0).astype(BF16)
            lift = lift + dot(scaled, hot, ((0,), (0,)))
        lifts.append(lift.astype(BF16))
    lift = jnp.concatenate(lifts, axis=1)
    block = 512
    for n in range(half // block):
        span = slice(n * block, (n + 1) * block)
        rows_in = jnp.concatenate([ref[:tokens, span] for ref in readout_refs], axis=0)
        pack_ref[:, :, span] = dot(lift, rows_in).astype(BF16).reshape(part, rank, block)


def weigh(logs, readouts, latents, picked, gains, rank, tokens, chunks):
    part = LINE * LINE
    half = readouts[0].shape[1]
    return pl.pallas_call(
        functools.partial(weigh_body, chunks, tokens),
        out_shape=[
            jax.ShapeDtypeStruct((1, tokens), F32),
            jax.ShapeDtypeStruct((part, rank, half + latents.shape[1]), BF16),
        ],
        compiler_params=pltpu.CompilerParams(vmem_limit_bytes=20 * 1024 * 1024),
        name="weigh_tokens",
    )(*logs, *readouts, latents, picked, gains)


def gradients_body(groups, chunks, place_ref, packed_ref, *refs):
    hid_refs, (grad_a_ref, grad_b_ref) = refs[:-2], refs[-2:]
    rank, half = grad_b_ref.shape
    part = packed_ref.shape[0]
    block = 256
    for n in range(half // block):
        span = slice(n * block, (n + 1) * block)
        grad_b_ref[:, span] = jnp.sum(packed_ref[:, :, span].astype(F32), axis=0)
    result = jnp.zeros(grad_a_ref.shape, F32)
    at = 0
    for hid_ref in hid_refs:
        rows = hid_ref.shape[0]
        count = rows // groups
        stacks = []
        for c in range(count // ROWS):
            stack = [packed_ref[:, step * LINE + at + c, half:] for step in range(LINE)]
            stacks.append(jnp.concatenate(stack, axis=0))
        at += count // ROWS
        shape = (rows, LINE * part)
        group, col = iota(shape, 0) // count, iota(shape, 1)
        block_of = (place_ref[1] + LINE - col // part) % LINE
        pick = ones_where(group == (col % part) * LINE + block_of)
        back = dot(pick, jnp.concatenate(stacks, axis=1))
        back = jnp.where(own_lanes(rows, rank, count), back, 0.0).astype(BF16)
        total = dot(back, hid_ref[...], ((0,), (0,)))
        for s in range(count):
            result = result + total[s * rank : (s + 1) * rank]
    grad_a_ref[...] = result


def gradients(place, packed, hidden, groups, chunks):
    rank = packed.shape[1]
    half = packed.shape[2] - ROWS * rank
    hidden_units = hidden[0].shape[1]
    args = (packed, *hidden)
    outs = [
        jax.ShapeDtypeStruct((rank, hidden_units), F32),
        jax.ShapeDtypeStruct((rank, half), F32),
    ]
    return pl.pallas_call(
        functools.partial(gradients_body, groups, chunks),
        grid_spec=pltpu.PrefetchScalarGridSpec(
            num_scalar_prefetch=1,
            grid=(1,),
            in_specs=[full(x.shape) for x in args],
            out_specs=[full(x.shape) for x in outs],
        ),
        out_shape=outs,
        compiler_params=pltpu.CompilerParams(vmem_limit_bytes=20 * 1024 * 1024),
        name="adapter_gradients",
    )(place, *args)


def swap(payload):
    return lax.ppermute(payload, "narrow", [(0, 1), (1, 0)])


def moved(payload, groups, stride, step):
    if step == 0:
        return payload
    moves = []
    for i in range(groups):
        at = i // stride % LINE
        moves.append((i, i + ((at + step) % LINE - at) * stride))
    return lax.ppermute(payload, "wide", moves)


def exchange(payload, among=None):
    return lax.all_to_all(
        payload, "wide", split_axis=0, concat_axis=0, tiled=True, axis_index_groups=among
    )


def on_device(
    hidden_in,
    readout,
    route_ids,
    route_weights,
    forget_mask,
    gate_proj,
    up_proj,
    adapter_a,
    adapter_b,
):
    groups = lax.axis_size("wide")
    pairs = lax.axis_size("narrow")
    tokens, picks = route_ids.shape
    features = hidden_in.shape[1]
    half = features // pairs
    rank = adapter_a.shape[1]
    chunks = sum(PARTS) // ROWS
    side = lax.axis_index("narrow")
    wide = lax.axis_index("wide")
    place = [side, wide % LINE, wide // LINE**2, wide // LINE % LINE]
    place = jnp.stack(place).astype(jnp.int32)
    planes = [list(range(z, groups, LINE)) for z in range(LINE)]

    ids_t, gains_t = route_ids.T, route_weights.T
    own_b = lax.dynamic_slice_in_dim(adapter_b[0], side * half, half, 1)
    mask = jnp.broadcast_to(forget_mask.astype(BF16), (ROWS, tokens))
    info = jnp.concatenate([ids_t.astype(BF16), gains_t, mask], axis=1)
    info = jnp.pad(info, ((0, 0), (0, half - 3 * tokens)))
    own_readout = lax.dynamic_slice_in_dim(readout, side * half, half, 1)
    own_readout = jnp.concatenate([own_readout, info], axis=0)

    adapters = [moved(own_b, groups, LINE, step) for step in range(LINE)]
    adapters = jnp.concatenate(adapters, axis=0)
    sent = list(dispatch(place, ids_t, hidden_in, groups))
    sent[0], adapters = lax.optimization_barrier((sent[0], adapters))
    x = exchange(sent[0].reshape(groups, PARTS[0], half)).reshape(groups * PARTS[0], half)
    x, adapters, own_readout = lax.optimization_barrier((x, adapters, own_readout))
    adapters = [moved(adapters, groups, LINE**2, step) for step in range(LINE)]
    readouts = [moved(own_readout, groups, 1, step) for step in range(LINE)]
    acts, latents = experts_forward(place, x, swap(x), gate_proj, up_proj, adapter_a, groups)
    acts, adapters, readouts = lax.optimization_barrier((acts, adapters, readouts))
    hidden = [acts]
    projections = project(readouts, adapters, tokens)
    picked, gains = pick(place, projections, swap(projections), readouts, tokens, chunks)
    latents, picked = lax.optimization_barrier((exchange(latents, planes), picked))
    log_part, latents = rate(latents, swap(latents), picked, gains, chunks)
    logs = [moved(log_part, groups, 1, step) for step in range(LINE)]
    log_ratio, packed = weigh(logs, readouts, latents, picked, gains, rank, tokens, chunks)
    grad_a, part_b = gradients(place, exchange(packed, planes), hidden, groups, chunks)
    other_b = swap(part_b)
    grad_b = jnp.where(
        side == 0,
        jnp.concatenate([part_b, other_b], axis=1),
        jnp.concatenate([other_b, part_b], axis=1),
    )
    return (log_ratio.reshape(tokens), grad_a[None], grad_b[None])


def solution(mesh):
    return jax.shard_map(
        on_device,
        mesh=mesh,
        in_specs=(
            P("wide", None),
            P("wide", None),
            P("wide", None),
            P("wide", None),
            P("wide"),
            P("wide", None, "narrow"),
            P("wide", None, "narrow"),
            P("wide", None, "narrow"),
            P("wide", None, None),
        ),
        out_specs=(P("wide"), P("wide", None, "narrow"), P("wide", None, None)),
        check_vma=False,
    )
```

```python
import functools

import jax
import jax.numpy as jnp
from jax import lax
from jax.experimental import pallas as pl
from jax.experimental.pallas import tpu as pltpu
from jax.sharding import PartitionSpec as P

F32 = jnp.float32
BF16 = jnp.bfloat16
ROWS = 8
LINE = 4
PARTS = (16, 8)


def iota(shape, dim):
    return lax.broadcasted_iota(jnp.int32, shape, dim)


def ones_where(condition, dtype=BF16):
    return jnp.where(condition, 1.0, 0.0).astype(dtype)


def dot(a, b, dims=((1,), (0,)), precision=None):
    return lax.dot_general(a, b, (dims, ((), ())), precision=precision, preferred_element_type=F32)


def slot_of_token(ids_t, expert):
    tokens = ids_t.shape[1]
    match = matched(ids_t, jnp.ones(ids_t.shape, F32), expert)
    before = ones_where(iota((tokens, tokens), 0) < iota((tokens, tokens), 1))
    rank = dot(match.astype(BF16), before)
    return jnp.where(match > 0.0, rank, -1.0)


def matched(ids_t, values_t, expert):
    result = jnp.zeros(expert.shape, F32)
    for k in range(ids_t.shape[0]):
        result = result + jnp.where(ids_t[k : k + 1, :] == expert, values_t[k : k + 1, :], 0.0)
    return result


def spread(groups, slots=ROWS):
    shape = (groups * slots, groups)
    return ones_where(iota(shape, 0) // slots == iota(shape, 1))


def gathered(groups):
    shape = (groups, groups * ROWS)
    return ones_where(iota(shape, 1) // ROWS == iota(shape, 0))


def full(shape):
    return pl.BlockSpec(shape, lambda *_: (0,) * len(shape))


def own_lanes(rows, rank, slots=ROWS):
    shape = (rows, slots * rank)
    return iota(shape, 0) % slots == iota(shape, 1) // rank


def one_hot_slots(slots, first, count=ROWS):
    rows = slots.shape[0] * count
    wide = dot(spread(slots.shape[0], count), slots.astype(BF16))
    wanted = (iota((rows, slots.shape[1]), 0) % count + first).astype(F32)
    return jnp.where(wide == wanted, 1.0, 0.0)


def dispatch_body(experts, core_ref, ids_ref, rows_ref, *refs):
    out_refs, hot_refs = refs[: len(PARTS)], refs[len(PARTS) :]

    @pl.when(pl.program_id(0) == 0)
    def _():
        expert = iota((experts, ids_ref.shape[1]), 0).astype(F32)
        slots = slot_of_token(ids_ref[...].astype(F32), expert)
        first = 0
        for hot_ref, count in zip(hot_refs, PARTS):
            hot_ref[...] = one_hot_slots(slots, first, count).astype(BF16)
            first += count

    rows = rows_ref[...]
    for out_ref, hot_ref in zip(out_refs, hot_refs):
        out_ref[...] = dot(hot_ref[...], rows).astype(BF16)


def dispatch(core, ids_t, rows, experts):
    tokens, features = rows.shape
    half = features // 2
    block = min(512, half)
    steps = half // block
    sizes = [experts * count for count in PARTS]
    return pl.pallas_call(
        functools.partial(dispatch_body, experts),
        grid_spec=pltpu.PrefetchScalarGridSpec(
            num_scalar_prefetch=1,
            grid=(steps,),
            in_specs=[
                pl.BlockSpec(ids_t.shape, lambda n, c: (0, 0)),
                pl.BlockSpec((tokens, block), lambda n, c: (0, c[0] * steps + n)),
            ],
            out_specs=[pl.BlockSpec((size, block), lambda n, c: (0, n)) for size in sizes],
            scratch_shapes=[pltpu.VMEM((size, tokens), BF16) for size in sizes],
        ),
        out_shape=[jax.ShapeDtypeStruct((size, half), BF16) for size in sizes],
        cost_estimate=pl.CostEstimate(
            flops=2 * sum(sizes) * tokens * half,
            bytes_accessed=2 * sum(sizes) * half,
            transcendentals=0,
        ),
        compiler_params=pltpu.CompilerParams(vmem_limit_bytes=58 * 1024 * 1024),
        name="dispatch_rows",
    )(core, ids_t, rows)


def experts_body(groups, count, steps, last, core_ref, own_ref, other_ref, go_ref, gx_ref, uo_ref, ux_ref, a_ref, *refs):
    before_refs, (hid_ref, lat_ref, acc_ref) = refs[:-3], refs[-3:]
    n = pl.program_id(0)
    own, other = own_ref[...], other_ref[...]
    gate = dot(own, go_ref[0]) + dot(other, gx_ref[0])
    up = dot(own, uo_ref[0]) + dot(other, ux_ref[0])
    hidden = (gate / (1.0 + jnp.exp(-gate)) * up).astype(BF16)
    hid_ref[...] = hidden
    rank = a_ref.shape[1]
    tiled = jnp.concatenate([a_ref[0]] * count, axis=0)
    part = dot(hidden, tiled, ((1,), (1,)))

    @pl.when(n == 0)
    def _():
        acc_ref[...] = part

    @pl.when(n > 0)
    def _():
        acc_ref[...] = acc_ref[...] + part

    @pl.when(n == steps - 1)
    def _():
        rows = groups * count
        mine = jnp.where(own_lanes(rows, rank, count), acc_ref[...], 0.0).astype(BF16)
        width = ROWS * rank
        shape = (groups // LINE, rows)
        for step in range(LINE):
            block = lax.rem(core_ref[1] + LINE - step, LINE)
            pick = ones_where(iota(shape, 1) // count == iota(shape, 0) * LINE + block)
            now = dot(pick, mine).astype(BF16)
            if last:
                at = step * LINE
                for piece in [ref[step] for ref in before_refs] + [now]:
                    for c in range(piece.shape[1] // width):
                        lat_ref[:, at, :] = piece[:, c * width : (c + 1) * width]
                        at += 1
                for c in range(at, (step + 1) * LINE):
                    lat_ref[:, c, :] = jnp.zeros((groups // LINE, width), BF16)
            else:
                lat_ref[step] = now


def experts_forward(core, own, other, gate, up, adapter_a, before, groups, last):
    rows, half = own.shape
    count = rows // groups
    hidden_units = gate.shape[2]
    rank = adapter_a.shape[1]
    block = min(256, hidden_units)
    steps = hidden_units // block
    width = count * rank
    mine = pl.BlockSpec((1, half, block), lambda n, c: (0, c[0], n))
    theirs = pl.BlockSpec((1, half, block), lambda n, c: (0, 1 - c[0], n))
    whole = pl.BlockSpec((rows, half), lambda n, c: (0, 0))
    in_specs = [whole, whole, mine, theirs, mine, theirs, pl.BlockSpec((1, rank, block), lambda n, c: (0, 0, n))]
    in_specs += [full(x.shape) for x in before]
    lines = groups // LINE
    out = (lines, LINE * LINE, ROWS * rank) if last else (LINE, lines, width)
    return pl.pallas_call(
        functools.partial(experts_body, groups, count, steps, last),
        grid_spec=pltpu.PrefetchScalarGridSpec(
            num_scalar_prefetch=1,
            grid=(steps,),
            in_specs=in_specs,
            out_specs=[
                pl.BlockSpec((rows, block), lambda n, c: (0, n)),
                full(out),
            ],
            scratch_shapes=[pltpu.VMEM((rows, width), F32)],
        ),
        out_shape=[
            jax.ShapeDtypeStruct((rows, hidden_units), BF16),
            jax.ShapeDtypeStruct(out, BF16),
        ],
        cost_estimate=pl.CostEstimate(
            flops=8 * rows * half * hidden_units,
            bytes_accessed=8 * half * hidden_units + 4 * rows * half,
            transcendentals=rows * hidden_units,
        ),
        compiler_params=pltpu.CompilerParams(vmem_limit_bytes=48 * 1024 * 1024),
        name="experts_forward",
    )(core, own, other, gate, gate, up, up, adapter_a, *before)


def project_body(tokens, *refs):
    readout_refs, adapter_refs, out_ref = refs[:LINE], refs[LINE : 2 * LINE], refs[2 * LINE]
    adapters = jnp.concatenate([ref[...] for ref in adapter_refs], axis=0)
    for step, ref in enumerate(readout_refs):
        out_ref[step * tokens : (step + 1) * tokens, :] = dot(ref[:tokens, :], adapters, ((1,), (1,)))


def project(readouts, adapters, tokens):
    half = readouts[0].shape[1]
    width = LINE * adapters[0].shape[0]
    return pl.pallas_call(
        functools.partial(project_body, tokens),
        out_shape=jax.ShapeDtypeStruct((LINE * tokens, width), F32),
        cost_estimate=pl.CostEstimate(
            flops=2 * LINE * tokens * width * half,
            bytes_accessed=2 * half * (LINE * tokens + width),
            transcendentals=0,
        ),
        compiler_params=pltpu.CompilerParams(vmem_limit_bytes=16 * 1024 * 1024),
        name="project_readout",
    )(*readouts, *adapters)


def pick_body(tokens, chunks, place_ref, own_ref, other_ref, *refs):
    info_refs, (picked_ref, gain_ref) = refs[:LINE], refs[LINE:]
    every = own_ref.shape[1]
    part = LINE * LINE
    rank = every // part
    rows, width = part * ROWS, ROWS * rank
    lanes = own_lanes(rows, rank)
    shape = (rows, every)
    line = iota(shape, 0) // ROWS
    back = iota(shape, 1) // rank
    row_y, row_x = line // LINE, line % LINE
    col_y = (place_ref[2] + LINE - back // LINE) % LINE
    col_x = (place_ref[3] + LINE - back % LINE) % LINE
    own_expert = (row_y == col_y) & (row_x == col_x)
    fold = ones_where(iota((every, width), 0) % rank == iota((every, width), 1) % rank)
    expert = (iota((part, tokens), 0) * LINE + place_ref[1]).astype(F32)
    for step, info_ref in enumerate(info_refs):
        ids_t = info_ref[:, :tokens].astype(F32)
        gains_t = info_ref[:, tokens : 2 * tokens].astype(F32)
        slots = slot_of_token(ids_t, expert)
        gains = dot(spread(part), matched(ids_t, gains_t, expert).astype(BF16))
        span = slice(step * tokens, (step + 1) * tokens)
        projection = (own_ref[span, :] + other_ref[span, :]).astype(BF16)
        for c in range(chunks):
            hot = one_hot_slots(slots, c * ROWS)
            at = step * chunks + c
            gain_ref[at * rows : (at + 1) * rows, :] = (hot * gains).astype(BF16)
            picked = jnp.where(own_expert, dot(hot.astype(BF16), projection), 0.0).astype(BF16)
            placed = jnp.where(lanes, dot(picked, fold), 0.0).astype(BF16)
            picked_ref[at * part : (at + 1) * part, :] = dot(gathered(part), placed)


def pick(place, own, other, infos, tokens, chunks):
    part = LINE * LINE
    width = ROWS * (own.shape[1] // part)
    count = LINE * chunks * part
    outs = [
        jax.ShapeDtypeStruct((count, width), F32),
        jax.ShapeDtypeStruct((count * ROWS, tokens), BF16),
    ]
    info = pl.BlockSpec((ROWS, 3 * tokens), lambda n, c: (tokens // ROWS, 0))
    return pl.pallas_call(
        functools.partial(pick_body, tokens, chunks),
        grid_spec=pltpu.PrefetchScalarGridSpec(
            num_scalar_prefetch=1,
            grid=(1,),
            in_specs=[full(own.shape), full(other.shape)] + [info] * LINE,
            out_specs=[full(x.shape) for x in outs],
        ),
        out_shape=outs,
        compiler_params=pltpu.CompilerParams(vmem_limit_bytes=16 * 1024 * 1024),
        name="pick_projections",
    )(place, own, other, *infos)


def rate_body(chunks, own_ref, other_ref, picked_ref, gain_ref, log_ref, latent_ref):
    part, _, width = own_ref.shape
    rank = width // ROWS
    pieces = []
    for step in range(LINE):
        for c in range(chunks):
            row = step * LINE + c
            pieces.append(own_ref[:, row, :].astype(F32) + other_ref[:, row, :].astype(F32))
    latent = jnp.concatenate(pieces, axis=0).astype(BF16)
    latent_ref[...] = latent
    same = ones_where(iota((width, width), 0) // rank == iota((width, width), 1) // rank, F32)
    score = dot(latent.astype(F32) * picked_ref[...], same, precision=lax.Precision.HIGHEST)
    rows = part * ROWS
    lanes = own_lanes(rows, rank) & (iota((rows, width), 1) % rank == 0)
    tokens = gain_ref.shape[1]
    log_ref[...] = jnp.zeros(log_ref.shape, F32)
    for step in range(LINE):
        total = jnp.zeros((1, tokens), F32)
        for c in range(chunks):
            at = step * chunks + c
            wide = dot(spread(part), score[at * part : (at + 1) * part].astype(BF16))
            column = jnp.sum(jnp.where(lanes, wide, 0.0), axis=1, keepdims=True)
            gain = gain_ref[at * rows : (at + 1) * rows, :].astype(F32)
            total = total + jnp.sum(gain * column, axis=0, keepdims=True)
        log_ref[step : step + 1, :] = total


def rate(own, other, picked, gains, chunks):
    return pl.pallas_call(
        functools.partial(rate_body, chunks),
        out_shape=[
            jax.ShapeDtypeStruct((ROWS, gains.shape[1]), F32),
            jax.ShapeDtypeStruct(picked.shape, BF16),
        ],
        compiler_params=pltpu.CompilerParams(vmem_limit_bytes=12 * 1024 * 1024),
        name="rate_tokens",
    )(own, other, picked, gains)


def weigh_body(chunks, tokens, *refs):
    log_refs, readout_refs = refs[:LINE], refs[LINE : 2 * LINE]
    latent_ref, picked_ref, gain_ref, out_ref, pack_ref = refs[2 * LINE :]
    part, rank, _ = pack_ref.shape
    half = readout_refs[0].shape[1]
    width = latent_ref.shape[1]
    rows = part * ROWS
    every = part * rank
    lanes = own_lanes(rows, rank)
    spread_rows = spread(part)
    tile = ones_where(iota((width, every), 0) % rank == iota((width, every), 1) % rank)
    own_expert = iota((rows, every), 0) // ROWS == iota((rows, every), 1) // rank
    lifts = []
    pack_ref[:, :, half:] = jnp.zeros((part, rank, width), BF16)
    for step in range(LINE):
        total = log_refs[0][step : step + 1, :]
        for back in range(1, LINE):
            at = (step - back) % LINE
            total = total + log_refs[back][at : at + 1, :]
        if step == 0:
            out_ref[...] = total
        mask = readout_refs[step][tokens : tokens + 1, 2 * tokens : 3 * tokens].astype(F32)
        coefficient = 2.0 * mask / (1.0 + jnp.exp(-total))
        lift = jnp.zeros((every, tokens), F32)
        for c in range(chunks):
            at = step * chunks + c
            span = slice(at * rows, (at + 1) * rows)
            gain = gain_ref[span, :].astype(F32)
            hot = ones_where(gain > 0.0)
            weight = (gain * coefficient).astype(BF16).astype(F32)
            column = jnp.sum(weight, axis=1, keepdims=True)
            placed = jnp.where(lanes, column, 0.0).astype(BF16)
            weight = dot(gathered(part), placed)
            few = slice(at * part, (at + 1) * part)
            pack_ref[:, step * LINE + c, half:] = (weight * picked_ref[few, :]).astype(BF16)
            scaled = (weight * latent_ref[few, :].astype(F32)).astype(BF16)
            scaled = jnp.where(lanes, dot(spread_rows, scaled), 0.0).astype(BF16)
            scaled = jnp.where(own_expert, dot(scaled, tile), 0.0).astype(BF16)
            lift = lift + dot(scaled, hot, ((0,), (0,)))
        lifts.append(lift.astype(BF16))
    lift = jnp.concatenate(lifts, axis=1)
    block = 512
    for n in range(half // block):
        span = slice(n * block, (n + 1) * block)
        rows_in = jnp.concatenate([ref[:tokens, span] for ref in readout_refs], axis=0)
        pack_ref[:, :, span] = dot(lift, rows_in).astype(BF16).reshape(part, rank, block)


def weigh(logs, readouts, latents, picked, gains, rank, tokens, chunks):
    part = LINE * LINE
    half = readouts[0].shape[1]
    return pl.pallas_call(
        functools.partial(weigh_body, chunks, tokens),
        out_shape=[
            jax.ShapeDtypeStruct((1, tokens), F32),
            jax.ShapeDtypeStruct((part, rank, half + latents.shape[1]), BF16),
        ],
        compiler_params=pltpu.CompilerParams(vmem_limit_bytes=20 * 1024 * 1024),
        name="weigh_tokens",
    )(*logs, *readouts, latents, picked, gains)


def gradients_body(groups, chunks, place_ref, packed_ref, *refs):
    hid_refs, (grad_a_ref, grad_b_ref) = refs[:-2], refs[-2:]
    rank, half = grad_b_ref.shape
    part = packed_ref.shape[0]
    block = 256
    for n in range(half // block):
        span = slice(n * block, (n + 1) * block)
        grad_b_ref[:, span] = jnp.sum(packed_ref[:, :, span].astype(F32), axis=0)
    result = jnp.zeros(grad_a_ref.shape, F32)
    at = 0
    for hid_ref in hid_refs:
        rows = hid_ref.shape[0]
        count = rows // groups
        stacks = []
        for c in range(count // ROWS):
            stack = [packed_ref[:, step * LINE + at + c, half:] for step in range(LINE)]
            stacks.append(jnp.concatenate(stack, axis=0))
        at += count // ROWS
        shape = (rows, LINE * part)
        group, col = iota(shape, 0) // count, iota(shape, 1)
        block_of = (place_ref[1] + LINE - col // part) % LINE
        pick = ones_where(group == (col % part) * LINE + block_of)
        back = dot(pick, jnp.concatenate(stacks, axis=1))
        back = jnp.where(own_lanes(rows, rank, count), back, 0.0).astype(BF16)
        total = dot(back, hid_ref[...], ((0,), (0,)))
        for s in range(count):
            result = result + total[s * rank : (s + 1) * rank]
    grad_a_ref[...] = result


def gradients(place, packed, hidden, groups, chunks):
    rank = packed.shape[1]
    half = packed.shape[2] - ROWS * rank
    hidden_units = hidden[0].shape[1]
    args = (packed, *hidden)
    outs = [
        jax.ShapeDtypeStruct((rank, hidden_units), F32),
        jax.ShapeDtypeStruct((rank, half), F32),
    ]
    return pl.pallas_call(
        functools.partial(gradients_body, groups, chunks),
        grid_spec=pltpu.PrefetchScalarGridSpec(
            num_scalar_prefetch=1,
            grid=(1,),
            in_specs=[full(x.shape) for x in args],
            out_specs=[full(x.shape) for x in outs],
        ),
        out_shape=outs,
        compiler_params=pltpu.CompilerParams(vmem_limit_bytes=20 * 1024 * 1024),
        name="adapter_gradients",
    )(place, *args)


def swap(payload):
    return lax.ppermute(payload, "narrow", [(0, 1), (1, 0)])


def moved(payload, groups, stride, step):
    if step == 0:
        return payload
    moves = []
    for i in range(groups):
        at = i // stride % LINE
        moves.append((i, i + ((at + step) % LINE - at) * stride))
    return lax.ppermute(payload, "wide", moves)


def exchange(payload, among=None):
    return lax.all_to_all(
        payload, "wide", split_axis=0, concat_axis=0, tiled=True, axis_index_groups=among
    )


def on_device(
    hidden_in,
    readout,
    route_ids,
    route_weights,
    forget_mask,
    gate_proj,
    up_proj,
    adapter_a,
    adapter_b,
):
    groups = lax.axis_size("wide")
    pairs = lax.axis_size("narrow")
    tokens, picks = route_ids.shape
    features = hidden_in.shape[1]
    half = features // pairs
    rank = adapter_a.shape[1]
    chunks = sum(PARTS) // ROWS
    side = lax.axis_index("narrow")
    wide = lax.axis_index("wide")
    place = [side, wide % LINE, wide // LINE**2, wide // LINE % LINE]
    place = jnp.stack(place).astype(jnp.int32)
    planes = [list(range(z, groups, LINE)) for z in range(LINE)]

    ids_t, gains_t = route_ids.T, route_weights.T
    own_b = lax.dynamic_slice_in_dim(adapter_b[0], side * half, half, 1)
    mask = jnp.broadcast_to(forget_mask.astype(BF16), (ROWS, tokens))
    info = jnp.concatenate([ids_t.astype(BF16), gains_t, mask], axis=1)
    info = jnp.pad(info, ((0, 0), (0, half - 3 * tokens)))
    own_readout = lax.dynamic_slice_in_dim(readout, side * half, half, 1)
    own_readout = jnp.concatenate([own_readout, info], axis=0)

    adapters = [moved(own_b, groups, LINE, step) for step in range(LINE)]
    adapters = jnp.concatenate(adapters, axis=0)
    sent = list(dispatch(place, ids_t, hidden_in, groups))
    sent[0], adapters = lax.optimization_barrier((sent[0], adapters))
    x = exchange(sent[0].reshape(groups, PARTS[0], half)).reshape(groups * PARTS[0], half)
    y = exchange(sent[1].reshape(groups, PARTS[1], half)).reshape(groups * PARTS[1], half)
    acts, sums = experts_forward(
        place, x, swap(x), gate_proj, up_proj, adapter_a, [], groups, False
    )
    adapters = [moved(adapters, groups, LINE**2, step) for step in range(LINE)]
    y, acts, adapters[1], adapters[3], own_readout = lax.optimization_barrier(
        (y, acts, adapters[1], adapters[3], own_readout)
    )
    readouts = [moved(own_readout, groups, 1, step) for step in range(LINE)]
    last_acts, latents = experts_forward(
        place, y, swap(y), gate_proj, up_proj, adapter_a, [sums], groups, True
    )
    last_acts, adapters[2], readouts = lax.optimization_barrier((last_acts, adapters[2], readouts))
    hidden = [acts, last_acts]
    projections = project(readouts, adapters, tokens)
    picked, gains = pick(place, projections, swap(projections), readouts, tokens, chunks)
    latents, picked = lax.optimization_barrier((exchange(latents, planes), picked))
    log_part, latents = rate(latents, swap(latents), picked, gains, chunks)
    logs = [moved(log_part, groups, 1, step) for step in range(LINE)]
    log_ratio, packed = weigh(logs, readouts, latents, picked, gains, rank, tokens, chunks)
    grad_a, part_b = gradients(place, exchange(packed, planes), hidden, groups, chunks)
    other_b = swap(part_b)
    grad_b = jnp.where(
        side == 0,
        jnp.concatenate([part_b, other_b], axis=1),
        jnp.concatenate([other_b, part_b], axis=1),
    )
    return (log_ratio.reshape(tokens), grad_a[None], grad_b[None])


def solution(mesh):
    return jax.shard_map(
        on_device,
        mesh=mesh,
        in_specs=(
            P("wide", None),
            P("wide", None),
            P("wide", None),
            P("wide", None),
            P("wide"),
            P("wide", None, "narrow"),
            P("wide", None, "narrow"),
            P("wide", None, "narrow"),
            P("wide", None, None),
        ),
        out_specs=(P("wide"), P("wide", None, "narrow"), P("wide", None, None)),
        check_vma=False,
    )
```

```python
import functools

import jax
import jax.numpy as jnp
from jax import lax
from jax.experimental import pallas as pl
from jax.experimental.pallas import tpu as pltpu
from jax.sharding import PartitionSpec as P

F32 = jnp.float32
BF16 = jnp.bfloat16
ROWS = 8
LINE = 4
PARTS = (16, 8)


def iota(shape, dim):
    return lax.broadcasted_iota(jnp.int32, shape, dim)


def ones_where(condition, dtype=BF16):
    return jnp.where(condition, 1.0, 0.0).astype(dtype)


def dot(a, b, dims=((1,), (0,)), precision=None):
    return lax.dot_general(a, b, (dims, ((), ())), precision=precision, preferred_element_type=F32)


def slot_of_token(ids_t, expert):
    tokens = ids_t.shape[1]
    match = matched(ids_t, jnp.ones(ids_t.shape, F32), expert)
    before = ones_where(iota((tokens, tokens), 0) < iota((tokens, tokens), 1))
    rank = dot(match.astype(BF16), before)
    return jnp.where(match > 0.0, rank, -1.0)


def matched(ids_t, values_t, expert):
    result = jnp.zeros(expert.shape, F32)
    for k in range(ids_t.shape[0]):
        result = result + jnp.where(ids_t[k : k + 1, :] == expert, values_t[k : k + 1, :], 0.0)
    return result


def spread(groups, slots=ROWS):
    shape = (groups * slots, groups)
    return ones_where(iota(shape, 0) // slots == iota(shape, 1))


def gathered(groups):
    shape = (groups, groups * ROWS)
    return ones_where(iota(shape, 1) // ROWS == iota(shape, 0))


def full(shape):
    return pl.BlockSpec(shape, lambda *_: (0,) * len(shape))


def own_lanes(rows, rank, slots=ROWS):
    shape = (rows, slots * rank)
    return iota(shape, 0) % slots == iota(shape, 1) // rank


def one_hot_slots(slots, first, count=ROWS):
    rows = slots.shape[0] * count
    wide = dot(spread(slots.shape[0], count), slots.astype(BF16))
    wanted = (iota((rows, slots.shape[1]), 0) % count + first).astype(F32)
    return jnp.where(wide == wanted, 1.0, 0.0)


def dispatch_body(experts, core_ref, ids_ref, rows_ref, *refs):
    out_refs, hot_refs = refs[: len(PARTS)], refs[len(PARTS) :]

    @pl.when(pl.program_id(0) == 0)
    def _():
        expert = iota((experts, ids_ref.shape[1]), 0).astype(F32)
        slots = slot_of_token(ids_ref[...].astype(F32), expert)
        first = 0
        for hot_ref, count in zip(hot_refs, PARTS):
            hot_ref[...] = one_hot_slots(slots, first, count).astype(BF16)
            first += count

    rows = rows_ref[...]
    for out_ref, hot_ref in zip(out_refs, hot_refs):
        out_ref[...] = dot(hot_ref[...], rows).astype(BF16)


def dispatch(core, ids_t, rows, experts):
    tokens, features = rows.shape
    half = features // 2
    block = min(512, half)
    steps = half // block
    sizes = [experts * count for count in PARTS]
    return pl.pallas_call(
        functools.partial(dispatch_body, experts),
        grid_spec=pltpu.PrefetchScalarGridSpec(
            num_scalar_prefetch=1,
            grid=(steps,),
            in_specs=[
                pl.BlockSpec(ids_t.shape, lambda n, c: (0, 0)),
                pl.BlockSpec((tokens, block), lambda n, c: (0, c[0] * steps + n)),
            ],
            out_specs=[pl.BlockSpec((size, block), lambda n, c: (0, n)) for size in sizes],
            scratch_shapes=[pltpu.VMEM((size, tokens), BF16) for size in sizes],
        ),
        out_shape=[jax.ShapeDtypeStruct((size, half), BF16) for size in sizes],
        cost_estimate=pl.CostEstimate(
            flops=2 * sum(sizes) * tokens * half,
            bytes_accessed=2 * sum(sizes) * half,
            transcendentals=0,
        ),
        compiler_params=pltpu.CompilerParams(vmem_limit_bytes=58 * 1024 * 1024),
        name="dispatch_rows",
    )(core, ids_t, rows)


def experts_body(groups, count, steps, last, core_ref, own_ref, other_ref, go_ref, gx_ref, uo_ref, ux_ref, a_ref, *refs):
    before_refs, (hid_ref, lat_ref, acc_ref) = refs[:-3], refs[-3:]
    n = pl.program_id(0)
    own, other = own_ref[...], other_ref[...]
    gate = dot(own, go_ref[0]) + dot(other, gx_ref[0])
    up = dot(own, uo_ref[0]) + dot(other, ux_ref[0])
    hidden = (gate / (1.0 + jnp.exp(-gate)) * up).astype(BF16)
    hid_ref[...] = hidden
    rank = a_ref.shape[1]
    tiled = jnp.concatenate([a_ref[0]] * count, axis=0)
    part = dot(hidden, tiled, ((1,), (1,)))

    @pl.when(n == 0)
    def _():
        acc_ref[...] = part

    @pl.when(n > 0)
    def _():
        acc_ref[...] = acc_ref[...] + part

    @pl.when(n == steps - 1)
    def _():
        rows = groups * count
        mine = jnp.where(own_lanes(rows, rank, count), acc_ref[...], 0.0).astype(BF16)
        width = ROWS * rank
        shape = (groups // LINE, rows)
        for step in range(LINE):
            block = lax.rem(core_ref[1] + LINE - step, LINE)
            pick = ones_where(iota(shape, 1) // count == iota(shape, 0) * LINE + block)
            now = dot(pick, mine).astype(BF16)
            if last:
                at = step * LINE
                for piece in [ref[step] for ref in before_refs] + [now]:
                    for c in range(piece.shape[1] // width):
                        lat_ref[:, at, :] = piece[:, c * width : (c + 1) * width]
                        at += 1
                for c in range(at, (step + 1) * LINE):
                    lat_ref[:, c, :] = jnp.zeros((groups // LINE, width), BF16)
            else:
                lat_ref[step] = now


def experts_forward(core, own, other, gate, up, adapter_a, before, groups, last):
    rows, half = own.shape
    count = rows // groups
    hidden_units = gate.shape[2]
    rank = adapter_a.shape[1]
    block = min(256, hidden_units)
    steps = hidden_units // block
    width = count * rank
    mine = pl.BlockSpec((1, half, block), lambda n, c: (0, c[0], n))
    theirs = pl.BlockSpec((1, half, block), lambda n, c: (0, 1 - c[0], n))
    whole = pl.BlockSpec((rows, half), lambda n, c: (0, 0))
    in_specs = [whole, whole, mine, theirs, mine, theirs, pl.BlockSpec((1, rank, block), lambda n, c: (0, 0, n))]
    in_specs += [full(x.shape) for x in before]
    lines = groups // LINE
    out = (lines, LINE * LINE, ROWS * rank) if last else (LINE, lines, width)
    return pl.pallas_call(
        functools.partial(experts_body, groups, count, steps, last),
        grid_spec=pltpu.PrefetchScalarGridSpec(
            num_scalar_prefetch=1,
            grid=(steps,),
            in_specs=in_specs,
            out_specs=[
                pl.BlockSpec((rows, block), lambda n, c: (0, n)),
                full(out),
            ],
            scratch_shapes=[pltpu.VMEM((rows, width), F32)],
        ),
        out_shape=[
            jax.ShapeDtypeStruct((rows, hidden_units), BF16),
            jax.ShapeDtypeStruct(out, BF16),
        ],
        cost_estimate=pl.CostEstimate(
            flops=8 * rows * half * hidden_units,
            bytes_accessed=8 * half * hidden_units + 4 * rows * half,
            transcendentals=rows * hidden_units,
        ),
        compiler_params=pltpu.CompilerParams(vmem_limit_bytes=48 * 1024 * 1024),
        name="experts_forward",
    )(core, own, other, gate, gate, up, up, adapter_a, *before)


def project_body(tokens, *refs):
    readout_refs, adapter_refs, out_ref = refs[:LINE], refs[LINE : 2 * LINE], refs[2 * LINE]
    adapters = jnp.concatenate([ref[...] for ref in adapter_refs], axis=0)
    for step, ref in enumerate(readout_refs):
        out_ref[step * tokens : (step + 1) * tokens, :] = dot(ref[:tokens, :], adapters, ((1,), (1,)))


def project(readouts, adapters, tokens):
    half = readouts[0].shape[1]
    width = LINE * adapters[0].shape[0]
    return pl.pallas_call(
        functools.partial(project_body, tokens),
        out_shape=jax.ShapeDtypeStruct((LINE * tokens, width), F32),
        cost_estimate=pl.CostEstimate(
            flops=2 * LINE * tokens * width * half,
            bytes_accessed=2 * half * (LINE * tokens + width),
            transcendentals=0,
        ),
        compiler_params=pltpu.CompilerParams(vmem_limit_bytes=16 * 1024 * 1024),
        name="project_readout",
    )(*readouts, *adapters)


def pick_body(tokens, chunks, place_ref, own_ref, other_ref, *refs):
    info_refs, (picked_ref, gain_ref) = refs[:LINE], refs[LINE:]
    every = own_ref.shape[1]
    part = LINE * LINE
    rank = every // part
    rows, width = part * ROWS, ROWS * rank
    lanes = own_lanes(rows, rank)
    shape = (rows, every)
    line = iota(shape, 0) // ROWS
    back = iota(shape, 1) // rank
    row_y, row_x = line // LINE, line % LINE
    col_y = (place_ref[2] + LINE - back // LINE) % LINE
    col_x = (place_ref[3] + LINE - back % LINE) % LINE
    own_expert = (row_y == col_y) & (row_x == col_x)
    fold = ones_where(iota((every, width), 0) % rank == iota((every, width), 1) % rank)
    expert = (iota((part, tokens), 0) * LINE + place_ref[1]).astype(F32)
    for step, info_ref in enumerate(info_refs):
        ids_t = info_ref[:, :tokens].astype(F32)
        gains_t = info_ref[:, tokens : 2 * tokens].astype(F32)
        slots = slot_of_token(ids_t, expert)
        gains = dot(spread(part), matched(ids_t, gains_t, expert).astype(BF16))
        span = slice(step * tokens, (step + 1) * tokens)
        projection = (own_ref[span, :] + other_ref[span, :]).astype(BF16)
        for c in range(chunks):
            hot = one_hot_slots(slots, c * ROWS)
            at = step * chunks + c
            gain_ref[at * rows : (at + 1) * rows, :] = (hot * gains).astype(BF16)
            picked = jnp.where(own_expert, dot(hot.astype(BF16), projection), 0.0).astype(BF16)
            placed = jnp.where(lanes, dot(picked, fold), 0.0).astype(BF16)
            picked_ref[at * part : (at + 1) * part, :] = dot(gathered(part), placed)


def pick(place, own, other, infos, tokens, chunks):
    part = LINE * LINE
    width = ROWS * (own.shape[1] // part)
    count = LINE * chunks * part
    outs = [
        jax.ShapeDtypeStruct((count, width), F32),
        jax.ShapeDtypeStruct((count * ROWS, tokens), BF16),
    ]
    info = pl.BlockSpec((ROWS, 3 * tokens), lambda n, c: (tokens // ROWS, 0))
    return pl.pallas_call(
        functools.partial(pick_body, tokens, chunks),
        grid_spec=pltpu.PrefetchScalarGridSpec(
            num_scalar_prefetch=1,
            grid=(1,),
            in_specs=[full(own.shape), full(other.shape)] + [info] * LINE,
            out_specs=[full(x.shape) for x in outs],
        ),
        out_shape=outs,
        compiler_params=pltpu.CompilerParams(vmem_limit_bytes=16 * 1024 * 1024),
        name="pick_projections",
    )(place, own, other, *infos)


def rate_body(chunks, own_ref, other_ref, picked_ref, gain_ref, log_ref, latent_ref):
    part, _, width = own_ref.shape
    rank = width // ROWS
    pieces = []
    for step in range(LINE):
        for c in range(chunks):
            row = step * LINE + c
            pieces.append(own_ref[:, row, :].astype(F32) + other_ref[:, row, :].astype(F32))
    latent = jnp.concatenate(pieces, axis=0).astype(BF16)
    latent_ref[...] = latent
    same = ones_where(iota((width, width), 0) // rank == iota((width, width), 1) // rank, F32)
    score = dot(latent.astype(F32) * picked_ref[...], same, precision=lax.Precision.HIGHEST)
    rows = part * ROWS
    lanes = own_lanes(rows, rank) & (iota((rows, width), 1) % rank == 0)
    tokens = gain_ref.shape[1]
    log_ref[...] = jnp.zeros(log_ref.shape, F32)
    for step in range(LINE):
        total = jnp.zeros((1, tokens), F32)
        for c in range(chunks):
            at = step * chunks + c
            wide = dot(spread(part), score[at * part : (at + 1) * part].astype(BF16))
            column = jnp.sum(jnp.where(lanes, wide, 0.0), axis=1, keepdims=True)
            gain = gain_ref[at * rows : (at + 1) * rows, :].astype(F32)
            total = total + jnp.sum(gain * column, axis=0, keepdims=True)
        log_ref[step : step + 1, :] = total


def rate(own, other, picked, gains, chunks):
    return pl.pallas_call(
        functools.partial(rate_body, chunks),
        out_shape=[
            jax.ShapeDtypeStruct((ROWS, gains.shape[1]), F32),
            jax.ShapeDtypeStruct(picked.shape, BF16),
        ],
        compiler_params=pltpu.CompilerParams(vmem_limit_bytes=12 * 1024 * 1024),
        name="rate_tokens",
    )(own, other, picked, gains)


def weigh_body(chunks, tokens, *refs):
    log_refs, readout_refs = refs[:LINE], refs[LINE : 2 * LINE]
    latent_ref, picked_ref, gain_ref, out_ref, pack_ref = refs[2 * LINE :]
    part, rank, _ = pack_ref.shape
    half = readout_refs[0].shape[1]
    width = latent_ref.shape[1]
    rows = part * ROWS
    every = part * rank
    lanes = own_lanes(rows, rank)
    spread_rows = spread(part)
    tile = ones_where(iota((width, every), 0) % rank == iota((width, every), 1) % rank)
    own_expert = iota((rows, every), 0) // ROWS == iota((rows, every), 1) // rank
    lifts = []
    pack_ref[:, :, half:] = jnp.zeros((part, rank, width), BF16)
    for step in range(LINE):
        total = log_refs[0][step : step + 1, :]
        for back in range(1, LINE):
            at = (step - back) % LINE
            total = total + log_refs[back][at : at + 1, :]
        if step == 0:
            out_ref[...] = total
        mask = readout_refs[step][tokens : tokens + 1, 2 * tokens : 3 * tokens].astype(F32)
        coefficient = 2.0 * mask / (1.0 + jnp.exp(-total))
        lift = jnp.zeros((every, tokens), F32)
        for c in range(chunks):
            at = step * chunks + c
            span = slice(at * rows, (at + 1) * rows)
            gain = gain_ref[span, :].astype(F32)
            hot = ones_where(gain > 0.0)
            weight = (gain * coefficient).astype(BF16).astype(F32)
            column = jnp.sum(weight, axis=1, keepdims=True)
            placed = jnp.where(lanes, column, 0.0).astype(BF16)
            weight = dot(gathered(part), placed)
            few = slice(at * part, (at + 1) * part)
            pack_ref[:, step * LINE + c, half:] = (weight * picked_ref[few, :]).astype(BF16)
            scaled = (weight * latent_ref[few, :].astype(F32)).astype(BF16)
            scaled = jnp.where(lanes, dot(spread_rows, scaled), 0.0).astype(BF16)
            scaled = jnp.where(own_expert, dot(scaled, tile), 0.0).astype(BF16)
            lift = lift + dot(scaled, hot, ((0,), (0,)))
        lifts.append(lift.astype(BF16))
    lift = jnp.concatenate(lifts, axis=1)
    block = 512
    for n in range(half // block):
        span = slice(n * block, (n + 1) * block)
        rows_in = jnp.concatenate([ref[:tokens, span] for ref in readout_refs], axis=0)
        pack_ref[:, :, span] = dot(lift, rows_in).astype(BF16).reshape(part, rank, block)


def weigh(logs, readouts, latents, picked, gains, rank, tokens, chunks):
    part = LINE * LINE
    half = readouts[0].shape[1]
    return pl.pallas_call(
        functools.partial(weigh_body, chunks, tokens),
        out_shape=[
            jax.ShapeDtypeStruct((1, tokens), F32),
            jax.ShapeDtypeStruct((part, rank, half + latents.shape[1]), BF16),
        ],
        compiler_params=pltpu.CompilerParams(vmem_limit_bytes=20 * 1024 * 1024),
        name="weigh_tokens",
    )(*logs, *readouts, latents, picked, gains)


def gradients_body(groups, chunks, place_ref, packed_ref, *refs):
    hid_refs, (grad_a_ref, grad_b_ref) = refs[:-2], refs[-2:]
    rank, half = grad_b_ref.shape
    part = packed_ref.shape[0]
    block = 256
    for n in range(half // block):
        span = slice(n * block, (n + 1) * block)
        grad_b_ref[:, span] = jnp.sum(packed_ref[:, :, span].astype(F32), axis=0)
    result = jnp.zeros(grad_a_ref.shape, F32)
    at = 0
    for hid_ref in hid_refs:
        rows = hid_ref.shape[0]
        count = rows // groups
        stacks = []
        for c in range(count // ROWS):
            stack = [packed_ref[:, step * LINE + at + c, half:] for step in range(LINE)]
            stacks.append(jnp.concatenate(stack, axis=0))
        at += count // ROWS
        shape = (rows, LINE * part)
        group, col = iota(shape, 0) // count, iota(shape, 1)
        block_of = (place_ref[1] + LINE - col // part) % LINE
        pick = ones_where(group == (col % part) * LINE + block_of)
        back = dot(pick, jnp.concatenate(stacks, axis=1))
        back = jnp.where(own_lanes(rows, rank, count), back, 0.0).astype(BF16)
        total = dot(back, hid_ref[...], ((0,), (0,)))
        for s in range(count):
            result = result + total[s * rank : (s + 1) * rank]
    grad_a_ref[...] = result


def gradients(place, packed, hidden, groups, chunks):
    rank = packed.shape[1]
    half = packed.shape[2] - ROWS * rank
    hidden_units = hidden[0].shape[1]
    args = (packed, *hidden)
    outs = [
        jax.ShapeDtypeStruct((rank, hidden_units), F32),
        jax.ShapeDtypeStruct((rank, half), F32),
    ]
    return pl.pallas_call(
        functools.partial(gradients_body, groups, chunks),
        grid_spec=pltpu.PrefetchScalarGridSpec(
            num_scalar_prefetch=1,
            grid=(1,),
            in_specs=[full(x.shape) for x in args],
            out_specs=[full(x.shape) for x in outs],
        ),
        out_shape=outs,
        compiler_params=pltpu.CompilerParams(vmem_limit_bytes=20 * 1024 * 1024),
        name="adapter_gradients",
    )(place, *args)


def swap(payload):
    return lax.ppermute(payload, "narrow", [(0, 1), (1, 0)])


def moved(payload, groups, stride, step):
    if step == 0:
        return payload
    moves = []
    for i in range(groups):
        at = i // stride % LINE
        moves.append((i, i + ((at + step) % LINE - at) * stride))
    return lax.ppermute(payload, "wide", moves)


def exchange(payload, among=None):
    return lax.all_to_all(
        payload, "wide", split_axis=0, concat_axis=0, tiled=True, axis_index_groups=among
    )


def on_device(
    hidden_in,
    readout,
    route_ids,
    route_weights,
    forget_mask,
    gate_proj,
    up_proj,
    adapter_a,
    adapter_b,
):
    groups = lax.axis_size("wide")
    pairs = lax.axis_size("narrow")
    tokens, picks = route_ids.shape
    features = hidden_in.shape[1]
    half = features // pairs
    rank = adapter_a.shape[1]
    chunks = sum(PARTS) // ROWS
    side = lax.axis_index("narrow")
    wide = lax.axis_index("wide")
    place = [side, wide % LINE, wide // LINE**2, wide // LINE % LINE]
    place = jnp.stack(place).astype(jnp.int32)
    planes = [list(range(z, groups, LINE)) for z in range(LINE)]

    ids_t, gains_t = route_ids.T, route_weights.T
    own_b = lax.dynamic_slice_in_dim(adapter_b[0], side * half, half, 1)
    mask = jnp.broadcast_to(forget_mask.astype(BF16), (ROWS, tokens))
    info = jnp.concatenate([ids_t.astype(BF16), gains_t, mask], axis=1)
    info = jnp.pad(info, ((0, 0), (0, half - 3 * tokens)))
    own_readout = lax.dynamic_slice_in_dim(readout, side * half, half, 1)
    own_readout = jnp.concatenate([own_readout, info], axis=0)

    adapters = [moved(own_b, groups, LINE, step) for step in range(LINE)]
    adapters = jnp.concatenate(adapters, axis=0)
    sent = list(dispatch(place, ids_t, hidden_in, groups))
    sent[0], adapters = lax.optimization_barrier((sent[0], adapters))
    x = exchange(sent[0].reshape(groups, PARTS[0], half)).reshape(groups * PARTS[0], half)
    y = exchange(sent[1].reshape(groups, PARTS[1], half)).reshape(groups * PARTS[1], half)
    acts, sums = experts_forward(
        place, x, swap(x), gate_proj, up_proj, adapter_a, [], groups, False
    )
    adapters = [moved(adapters, groups, LINE**2, step) for step in range(LINE)]
    y, acts, adapters[1], adapters[3], own_readout = lax.optimization_barrier(
        (y, acts, adapters[1], adapters[3], own_readout)
    )
    readouts = [moved(own_readout, groups, 1, step) for step in range(LINE)]
    last_acts, latents = experts_forward(
        place, y, swap(y), gate_proj, up_proj, adapter_a, [sums], groups, True
    )
    latents, adapters[2], readouts = lax.optimization_barrier(
        (exchange(latents, planes), adapters[2], readouts)
    )
    hidden = [acts, last_acts]
    projections = project(readouts, adapters, tokens)
    picked, gains = pick(place, projections, swap(projections), readouts, tokens, chunks)
    log_part, latents = rate(latents, swap(latents), picked, gains, chunks)
    logs = [moved(log_part, groups, 1, step) for step in range(LINE)]
    log_ratio, packed = weigh(logs, readouts, latents, picked, gains, rank, tokens, chunks)
    grad_a, part_b = gradients(place, exchange(packed, planes), hidden, groups, chunks)
    other_b = swap(part_b)
    grad_b = jnp.where(
        side == 0,
        jnp.concatenate([part_b, other_b], axis=1),
        jnp.concatenate([other_b, part_b], axis=1),
    )
    return (log_ratio.reshape(tokens), grad_a[None], grad_b[None])


def solution(mesh):
    return jax.shard_map(
        on_device,
        mesh=mesh,
        in_specs=(
            P("wide", None),
            P("wide", None),
            P("wide", None),
            P("wide", None),
            P("wide"),
            P("wide", None, "narrow"),
            P("wide", None, "narrow"),
            P("wide", None, "narrow"),
            P("wide", None, None),
        ),
        out_specs=(P("wide"), P("wide", None, "narrow"), P("wide", None, None)),
        check_vma=False,
    )
```
